32 devices in a mesh: subj: 8 (over z, y), supp: 4 (over x, core).
Axes of the slice: x: 2, y: 2, z: 4, core: 2. Of those that a mesh axis runs over, the one named last changes fastest.
Arguments:
- observations: float32 [8192, 32], P('subj'), may hold values from -6 to 6
- noise_scale: float32 [8192, 32], P('subj'), may hold values from 0.3 to 1.5
- sample_times: int32 [8192, 32], P('subj'), may hold values from 0 to 127
- counts: int32 [32, 8192], P(None, 'subj'), may hold values from 0 to 3, as said below
- absorption: float32 [16384], P('supp'), may hold values from 1 to 4
- elimination: float32 [16384], P('supp'), may hold values from 0.05 to 0.5
- volume: float32 [16384], P('supp'), may hold values from 0.5 to 2
- weights: float32 [32, 16384], P(None, 'supp'), may hold values from 0.3 to 3
Outputs:
- new_weights: float32 [32, 16384], P(None, 'supp')
- loglik: float32 [32, 8192], P(None, 'subj')
The draws below stay inside these ranges and needn't reach their ends.
Inputs may be any that keep to these rules, and one draw needn't show every extreme that they name: `counts`: each of the 32 rows sums to 8192; in each row one eighth of the subjects have count 3, one eighth 2, three eighths 1 and three eighths 0.
All inputs are finite; a program needn't handle non-finite values.
Results may differ from the reference program's by a relative error of at most 0.0003.
Values sent between devices are 32-bit elements; how exact they have to be, the bound alone decides.
A program may use at most 64 MiB of HBM per device.

```python
import math
import jax
import jax.numpy as jnp
from jax import lax

K = 16384
J = 32
NT = 128
R = 32
ITERS = 2
NSUB = 8192


def draw_counts(key, part):
    eighth = NSUB // 8
    pattern = jnp.concatenate([jnp.full((eighth,), 3, jnp.int32), jnp.full((eighth,), 2, jnp.int32), jnp.full((3 * eighth,), 1, jnp.int32), jnp.zeros((NSUB - 5 * eighth,), jnp.int32)])
    row_keys = jax.random.split(jax.random.fold_in(key, 17), R)

    def one_row(row_key):
        order = jax.random.permutation(row_key, NSUB)
        return jnp.zeros((NSUB,), jnp.int32).at[order].set(pattern)
    return jax.vmap(one_row)(row_keys).astype(jnp.int32)


def with_ends(entries, rng, least, largest):
    index_at = [jax.random.randint(jax.random.fold_in(rng, axis), (), 0, length) for axis, length in enumerate(entries.shape)]
    main_axis = entries.shape.index(max(entries.shape))
    neighbour = index_at[:main_axis] + [(index_at[main_axis] + 1) % entries.shape[main_axis]] + index_at[main_axis + 1:]
    return entries.at[tuple(index_at)].set(least).at[tuple(neighbour)].set(largest)


def steps_of(rng, extent, pieces, low, top_value):
    def one(position, shards_of):
        heights = jax.random.uniform(jax.random.fold_in(jax.random.fold_in(rng, 6), position), (shards_of,), jnp.float32, low / len(pieces), top_value / len(pieces))
        return jnp.repeat(jnp.exp(heights), extent[position] // shards_of).reshape((-1,) + (1,) * (len(extent) - position - 1))

    loudness = one(*pieces[0])
    for cut in pieces[1:]:
        loudness = loudness * one(*cut)
    return loudness


def normal_values(stream_key, shape, deviation, most, pieces=(), kind=jnp.bfloat16):
    entries = deviation * jax.random.normal(stream_key, shape, jnp.float32)
    if pieces:
        entries = entries * steps_of(stream_key, shape, pieces, -0.22, 0.18)
    return jnp.clip(entries, -most, most).astype(kind)


def setup_inputs(seed: int = 0) -> dict:
    arg_keys = jax.random.split(jax.random.key(seed), 9)
    return {
        "observations": normal_values(arg_keys[0], (NSUB, J), 1.0, 6.0, ((0, 8),), jnp.float32),
        "noise_scale": jnp.clip(jnp.exp(math.log(1.5) - 1.60943787 * jax.random.uniform(arg_keys[1], (NSUB, J), jnp.float32) ** steps_of(arg_keys[1], (NSUB, J), ((0, 8),), -0.2, 0.2)), 0.3, 1.5),
        "sample_times": with_ends(jax.random.randint(arg_keys[2], (NSUB, J), 0, NT), jax.random.fold_in(arg_keys[2], 1), 0, NT - 1).astype(jnp.int32),
        "counts": draw_counts(jax.random.fold_in(arg_keys[8], 71), 0),
        "absorption": jnp.clip(jnp.exp(math.log(4.0) - 1.3862944 * jax.random.uniform(arg_keys[4], (K,), jnp.float32) ** steps_of(arg_keys[4], (K,), ((0, 4),), -0.2, 0.2)), 1.0, 4.0),
        "elimination": jnp.clip(jnp.exp(math.log(0.5) - 2.3025851 * jax.random.uniform(arg_keys[5], (K,), jnp.float32) ** steps_of(arg_keys[5], (K,), ((0, 4),), -0.2, 0.2)), 0.05, 0.5),
        "volume": jnp.clip(jnp.exp(math.log(2.0) - 1.3862944 * jax.random.uniform(arg_keys[6], (K,), jnp.float32) ** steps_of(arg_keys[6], (K,), ((0, 4),), -0.2, 0.2)), 0.5, 2.0),
        "weights": jnp.clip(jnp.exp(math.log(3.0) - 2.3025851 * jax.random.uniform(arg_keys[7], (R, K), jnp.float32) ** steps_of(arg_keys[7], (R, K), ((1, 4),), -0.2, 0.2)), 0.3, 3.0),
    }


exact_mode = lax.Precision.HIGHEST


def subject_features(observations, noise_scale, sample_times):
    precision_obs = 1.0 / (noise_scale * noise_scale)
    grid_index = jnp.arange(NT, dtype=jnp.int32)
    onehot = (sample_times[:, :, None] == grid_index[None, None, :]).astype(jnp.float32)
    linear_part = jnp.einsum("ij,ijg->ig", observations * precision_obs, onehot, precision=exact_mode)
    square_part = jnp.einsum("ij,ijg->ig", -0.5 * precision_obs, onehot, precision=exact_mode)
    offsets = -0.5 * jnp.sum(observations * observations * precision_obs, axis=1)
    log_scale = jnp.sum(jnp.log(noise_scale), axis=1)
    return jnp.concatenate([linear_part, square_part], axis=1), offsets, log_scale


def support_curves(absorption, elimination, volume):
    time_grid = (jnp.arange(NT, dtype=jnp.float32) + 1.0) * (24.0 / NT)
    amplitude = absorption / (volume * (absorption - elimination))
    curve_rows = amplitude[None, :] * (jnp.exp(-elimination[None, :] * time_grid[:, None]) - jnp.exp(-absorption[None, :] * time_grid[:, None]))
    return jnp.concatenate([curve_rows, curve_rows * curve_rows], axis=0)


def reference(observations, noise_scale, sample_times, counts, absorption, elimination, volume, weights):
    features, offsets, log_scale = subject_features(observations, noise_scale, sample_times)
    curves = support_curves(absorption, elimination, volume)
    block_size = math.gcd(NSUB, 1024)
    block_count = NSUB // block_size
    feat_blocks = features.reshape(block_count, block_size, 2 * NT)
    offset_blocks = offsets.reshape(block_count, block_size)

    def log_block(pair):
        return jnp.dot(pair[0], curves, precision=exact_mode) + pair[1][:, None]

    def tile_of(pair):
        log_lik = log_block(pair)
        return jnp.exp(log_lik - jnp.max(log_lik, axis=1)[:, None])

    peaks = lax.map(lambda pair: jnp.max(log_block(pair), axis=1), (feat_blocks, offset_blocks)).reshape(NSUB)
    count_float = counts.astype(jnp.float32)
    has_count = counts > 0
    current = weights
    loglik = jnp.zeros((R, NSUB), jnp.float32)
    for iteration in range(ITERS):
        mixture = lax.map(lambda pair: lax.dot_general(current, tile_of(pair), (((1,), (1,)), ((), ())), precision=exact_mode), (feat_blocks, offset_blocks))
        mixture = mixture.transpose(1, 0, 2).reshape(R, NSUB)
        if iteration == 0:
            loglik = (peaks[None, :] + jnp.log(mixture / K) - log_scale[None, :]) / J - 0.5 * math.log(2.0 * math.pi)
        resp_weight = jnp.where(has_count, count_float / jnp.where(has_count, mixture, 1.0), 0.0)
        resp_blocks = resp_weight.reshape(R, block_count, block_size).transpose(1, 0, 2)

        def accumulate(running, bundle):
            return running + jnp.dot(bundle[2], tile_of((bundle[0], bundle[1])), precision=exact_mode), None

        totals, unused = lax.scan(accumulate, jnp.zeros((R, K), jnp.float32), (feat_blocks, offset_blocks, resp_blocks))
        current = current * totals / NSUB
    return (current, loglik)
```

```python
import functools
import math

import jax
import jax.numpy as jnp
from jax import lax
from jax.experimental import pallas as pl
from jax.experimental.pallas import tpu as pltpu
from jax.sharding import PartitionSpec as P

NT = 128
HORIZON = 24.0
ITERS = 2
BLOCK = 256
KSTEP = 2048
CHUNKS = 4
FILL_STEPS = 2
GROUP = 32
PEAK_ROWS = 8
MIB = 1 << 20
F32 = jnp.float32
BF16 = jnp.bfloat16


def split(x):
    hi = x.astype(BF16)
    return hi, (x - hi.astype(F32)).astype(BF16)


def build_curves(absorption_ref, elimination_ref, volume_ref, curves, step):
    step_size = 512
    grid_rows = lax.broadcasted_iota(jnp.int32, (NT, step_size), 0).astype(F32)
    time_grid = (grid_rows + 1.0) * (HORIZON / NT)

    at = pl.ds(pl.multiple_of(step * step_size, step_size), step_size)
    rate_in = absorption_ref[:, at]
    rate_out = elimination_ref[:, at]
    amplitude = rate_in / (volume_ref[:, at] * (rate_in - rate_out))
    rows = amplitude * (jnp.exp(-rate_out * time_grid) - jnp.exp(-rate_in * time_grid))
    columns = rows.T
    for half, part in ((0, columns), (NT, columns * columns)):
        hi, lo = split(part)
        curves[at, half:half + NT] = hi
        curves[at, 2 * NT + half:3 * NT + half] = hi
        curves[at, 4 * NT + half:5 * NT + half] = lo


def block_mixture(obs, noise, times, curves, current, log_lik, tile_ref, columns):
    supports = log_lik.shape[0]
    steps = supports // KSTEP
    precision = 1.0 / (noise * noise)
    linear = obs * precision
    square = -0.5 * precision
    grid_index = lax.broadcasted_iota(jnp.int32, (NT, BLOCK), 0)
    linear_part = jnp.zeros((NT, BLOCK), F32)
    square_part = jnp.zeros((NT, BLOCK), F32)
    for j in range(obs.shape[0]):
        hit = times[j:j + 1, :] == grid_index
        linear_part = linear_part + jnp.where(hit, linear[j:j + 1, :], 0.0)
        square_part = square_part + jnp.where(hit, square[j:j + 1, :], 0.0)
    offset = -0.5 * jnp.sum(obs * obs * precision, axis=0, keepdims=True)
    log_scale = jnp.sum(jnp.log(noise), axis=0, keepdims=True)
    hi, lo = split(jnp.concatenate([linear_part, square_part], axis=0))
    features = jnp.concatenate([hi, lo, hi], axis=0)

    def one_log(step, peak):
        at = pl.ds(pl.multiple_of(step * KSTEP, KSTEP), KSTEP)
        part = jnp.dot(curves[at, :], features, preferred_element_type=F32)
        log_lik[at, :] = part
        return jnp.maximum(peak, jnp.max(part.reshape(KSTEP // 8, 8, BLOCK), axis=0))

    peak = lax.fori_loop(0, steps, one_log, jnp.full((8, BLOCK), -jnp.inf, F32))
    peak = jnp.max(peak, axis=0, keepdims=True)

    def one_tile(step, mix):
        at = pl.ds(pl.multiple_of(step * KSTEP, KSTEP), KSTEP)
        like = jnp.exp(log_lik[at, :] - peak).astype(BF16)
        tile_ref[at, columns] = like
        return mix + jnp.dot(current[:, at], like, preferred_element_type=F32)

    mix = lax.fori_loop(0, steps, one_tile, jnp.zeros((current.shape[0], BLOCK), F32))
    return mix, peak + offset, log_scale


def tile_kernel(obs_ref, noise_ref, times_ref, absorption_ref, elimination_ref, volume_ref,
                weights_ref, tile_ref, mix_ref, scale_ref, curves, current, log_lik):
    reps = weights_ref.shape[0]

    @pl.when(pl.program_id(0) == 0)
    def _():
        hi, lo = split(weights_ref[...])
        current[...] = jnp.concatenate([hi, lo], axis=0)
        @pl.loop(0, absorption_ref.shape[1] // 512)
        def _(step):
            build_curves(absorption_ref, elimination_ref, volume_ref, curves, step)

    mix, peak, log_scale = block_mixture(obs_ref[...], noise_ref[...], times_ref[...], curves, current,
                                         log_lik, tile_ref, slice(None))
    mix_ref[0, :reps, :] = mix[:reps] + mix[reps:]
    mix_ref[0, reps:, :] = jnp.broadcast_to(peak, (PEAK_ROWS, BLOCK))
    scale_ref[...] = jnp.broadcast_to(log_scale, (PEAK_ROWS, BLOCK))


def make_tile(obs, noise, times, absorption, elimination, volume, weights):
    samples, subjects = obs.shape
    reps, supports = weights.shape
    half = subjects // 2
    per_half = half // BLOCK
    by_subject = pl.BlockSpec((samples, BLOCK), lambda b: (0, b))
    whole = lambda shape: pl.BlockSpec(shape, lambda b: (0, 0))
    return pl.pallas_call(
        tile_kernel,
        grid=(subjects // BLOCK,),
        in_specs=[by_subject] * 3 + [whole((1, supports))] * 3 + [whole((reps, supports))],
        out_specs=[
            pl.BlockSpec((supports, BLOCK), lambda b: (0, b)),
            pl.BlockSpec((1, reps + PEAK_ROWS, BLOCK), lambda b: (b // per_half, 0, b % per_half)),
            pl.BlockSpec((PEAK_ROWS, BLOCK), lambda b: (0, b)),
        ],
        out_shape=[
            jax.ShapeDtypeStruct((supports, subjects), BF16),
            jax.ShapeDtypeStruct((2, reps + PEAK_ROWS, half), F32),
            jax.ShapeDtypeStruct((PEAK_ROWS, subjects), F32),
        ],
        scratch_shapes=[
            pltpu.VMEM((supports, 6 * NT), BF16),
            pltpu.VMEM((2 * reps, supports), BF16),
            pltpu.VMEM((supports, BLOCK), F32),
        ],
        compiler_params=pltpu.CompilerParams(vmem_limit_bytes=32 * MIB),
        name="make_tile",
    )(obs, noise, times, absorption, elimination, volume, weights)


def merge(mine, other, reps):
    peak_a, peak_b = mine[reps:], other[reps:]
    peak = jnp.maximum(peak_a, peak_b)
    scale_a, scale_b = jnp.exp(peak_a - peak)[:1], jnp.exp(peak_b - peak)[:1]
    return jnp.concatenate([mine[:reps] * scale_a + other[:reps] * scale_b, peak], axis=0)


def em_kernel(total_subjects, total_supports, ny, nz,
              obs_hbm, noise_hbm, times_hbm, absorption_hbm, elimination_hbm, volume_hbm, weights_hbm, counts_hbm,
              new_hbm, loglik_hbm,
              obs_v, noise_v, times_v, absorption_v, elimination_v, volume_v, weights_v, counts_v, load_sem,
              curves, current, linear_v, square_v, features_v, log_lik_even, log_lik_odd, tile, log_scale,
              new_v, loglik_v, out_sem,
              mix_own, mix_start, mix_pair, mix_near, mix_far, factor,
              sums, y_in, z_out, z_in, held,
              mix_send, mix_recv, y_send, y_recv, z_send, z_recv, gz_send, gz_recv, gy_send, gy_recv):
    samples = obs_v.shape[0]
    all_reps, subjects = counts_v.shape
    reps = all_reps
    half = subjects // 2
    per_half = half // BLOCK
    supports = weights_v.shape[1]
    width = supports // CHUNKS
    piece = width // (ny * nz)
    subj, supp = lax.axis_index("subj"), lax.axis_index("supp")
    y, z = lax.rem(subj, ny), lax.div(subj, ny)
    core = lax.rem(supp, 2)
    core_peer = {"subj": subj, "supp": supp + 1 - 2 * core}
    x_peer = {"subj": subj, "supp": lax.rem(supp + 2, 4)}
    y_peer = {"subj": subj + 1 - 2 * y, "supp": supp}
    z_at = [lax.rem(z + d, nz) for d in range(nz)]
    z_peers = [{"subj": z_at[d] * ny + y, "supp": supp} for d in range(nz)]
    sent, written = [], []

    def out(src, dst):
        copy = pltpu.make_async_copy(src, dst, out_sem.at[len(written)])
        copy.start()
        written.append(copy)

    mix_rows = lambda it: all_reps + PEAK_ROWS if it == 0 else all_reps

    loads = [pltpu.make_async_copy(src, dst, load_sem.at[k]) for k, (src, dst) in enumerate((
        (absorption_hbm, absorption_v), (elimination_hbm, elimination_v), (volume_hbm, volume_v),
        (weights_hbm, weights_v), (obs_hbm, obs_v), (noise_hbm, noise_v), (times_hbm, times_v),
        (counts_hbm, counts_v)))]
    for load in loads:
        load.start()

    def send(src, dst, send_sem, recv_sem, peer):
        copy = pltpu.make_async_remote_copy(
            src_ref=src, dst_ref=dst, send_sem=send_sem, recv_sem=recv_sem,
            device_id=peer, device_id_type=pl.DeviceIdType.MESH)
        copy.start()
        sent.append(copy)
        return copy

    barrier = pltpu.get_barrier_semaphore()
    peers = [core_peer, x_peer, y_peer] + z_peers[1:]
    for peer in peers:
        pl.semaphore_signal(barrier, inc=1, device_id=peer, device_id_type=pl.DeviceIdType.MESH)

    for load in loads:
        load.wait()
    hi, lo = split(weights_v[...])
    current[...] = jnp.concatenate([hi, lo], axis=0)
    blocks = subjects // BLOCK
    starts = [pl.multiple_of((1 - core) * half + b * BLOCK, BLOCK) for b in range(per_half)]
    starts += [pl.multiple_of(core * half + b * BLOCK, BLOCK) for b in range(per_half)]
    columns = [pl.ds(at, BLOCK) for at in starts]
    offsets = {}

    def prepare(b):
        obs, noise = obs_v[:, columns[b]], noise_v[:, columns[b]]
        precision = 1.0 / (noise * noise)
        linear = obs * precision
        linear_v[...] = linear
        square_v[...] = -0.5 * precision
        offsets[b] = -0.5 * jnp.sum(obs * linear, axis=0, keepdims=True)
        scale = jnp.sum(jnp.log(noise), axis=0, keepdims=True)
        log_scale[:, columns[b]] = jnp.broadcast_to(scale, (PEAK_ROWS, BLOCK))

    def feature_rows(b, step):
        features = features_v.at[b % 2]
        for k in range(NT // FILL_STEPS // GROUP):
            first_row = pl.multiple_of(step * (NT // FILL_STEPS) + k * GROUP, GROUP)
            index = lax.broadcasted_iota(jnp.int32, (GROUP, BLOCK), 0) + first_row
            linear_part = jnp.zeros((GROUP, BLOCK), F32)
            square_part = jnp.zeros((GROUP, BLOCK), F32)
            for j in range(samples):
                hit = times_v[j:j + 1, columns[b]] == index
                linear_part = linear_part + jnp.where(hit, linear_v[j:j + 1, :], 0.0)
                square_part = square_part + jnp.where(hit, square_v[j:j + 1, :], 0.0)
            for base, part in ((0, linear_part), (NT, square_part)):
                hi, lo = split(part)
                for slot, value in ((0, hi), (1, lo), (2, hi)):
                    at = pl.ds(pl.multiple_of(slot * 2 * NT + base + first_row, GROUP), GROUP)
                    features[at, :] = value

    fill_step = supports // FILL_STEPS
    logs = (log_lik_even, log_lik_odd)

    @pl.loop(0, supports // 512)
    def _(step):
        build_curves(absorption_v, elimination_v, volume_v, curves, step)

    prepare(0)

    @pl.loop(0, FILL_STEPS)
    def _(step):
        feature_rows(0, step)

    def fill_stage(b, peak_before):
        if b + 1 < blocks:
            prepare(b + 1)

        def one(step, carry):
            peak, mix = carry
            at = pl.ds(pl.multiple_of(step * fill_step, fill_step), fill_step)
            if b < blocks:
                part = jnp.dot(curves[at, :], features_v[b % 2], preferred_element_type=F32)
                logs[b % 2][at, :] = part
                peak = jnp.maximum(peak, jnp.max(part.reshape(fill_step // 8, 8, BLOCK), axis=0))
            if b > 0:
                like = jnp.exp(logs[(b - 1) % 2][at, :] - peak_before).astype(BF16)
                tile[at, columns[b - 1]] = like
                mix = mix + jnp.dot(current[:, at], like, preferred_element_type=F32)
            if b + 1 < blocks:
                feature_rows(b + 1, step)
            return peak, mix

        peak, mix = lax.fori_loop(0, FILL_STEPS, one, (
            jnp.full((8, BLOCK), -jnp.inf, F32), jnp.zeros((2 * all_reps, BLOCK), F32)))
        if b > 0:
            side = 1 - core if b - 1 < per_half else core
            within = slice((b - 1) % per_half * BLOCK, ((b - 1) % per_half + 1) * BLOCK)
            mix = mix[:all_reps] + mix[all_reps:]
            mix_start[0, side, :all_reps, within] = mix
            mix_start[0, side, all_reps:, within] = jnp.broadcast_to(
                peak_before + offsets[b - 1], (PEAK_ROWS, BLOCK))
        return jnp.max(peak, axis=0, keepdims=True)

    first = {}

    def start_exchange(it):
        to_send = pl.ds(0, mix_rows(it))
        first[it] = send(mix_start.at[it, 1 - core, to_send], mix_near.at[it, to_send], mix_send.at[it, 0],
                         mix_recv.at[it, 0], core_peer)

    peak = None
    for b in range(blocks + 1):
        peak = fill_stage(b, peak)
        if b == per_half:
            pl.semaphore_wait(barrier, len(peers))
            start_exchange(0)

    def stages_of(it):
        mixed = pl.ds(0, mix_rows(it))
        join = (lambda a, b: merge(a, b, reps)) if it == 0 else (lambda a, b: a + b)
        live = {}
        y_copies, z_copies, gz_copies, gy_copies = {}, {}, {}, {}

        def to_x():
            first[it].wait_recv()
            mix_pair[it, mixed] = join(mix_start[it, core, mixed], mix_near[it, mixed])
            live["x"] = send(mix_pair.at[it, mixed], mix_far.at[it, mixed], mix_send.at[it, 1],
                             mix_recv.at[it, 1], x_peer)

        def to_core():
            live["x"].wait_recv()
            mix_own[it, core, mixed] = join(mix_pair[it, mixed], mix_far[it, mixed])
            live["core"] = send(mix_own.at[it, core, mixed], mix_own.at[it, core, mixed], mix_send.at[it, 2],
                                mix_recv.at[it, 2], core_peer)

        def respond():
            live["core"].wait_recv()
            parts = []
            for side in range(2):
                columns = slice(side * half, (side + 1) * half)
                mixture = mix_own[it, side, :reps, :]
                if it == 0:
                    peak = mix_own[0, side, reps:, :]
                    factor[:, columns] = jnp.exp(mix_start[0, side, reps:, :] - peak)
                    loglik_v[:, columns] = (
                        peak[:1] + jnp.log(mixture / total_supports) - log_scale[:1, columns]
                    ) / samples - 0.5 * math.log(2.0 * math.pi)
                counts = counts_v[:, columns]
                drawn = counts > 0
                resp = jnp.where(drawn, counts.astype(F32) / jnp.where(drawn, mixture, 1.0), 0.0)
                parts.append(resp * factor[:1, columns])
            if it == 0:
                out(loglik_v, loglik_hbm)
            hi, lo = split(jnp.concatenate(parts, axis=1))
            live["resp"] = jnp.concatenate([hi, lo], axis=0)

        def compute(c):
            both = lax.dot_general(live["resp"], tile[c * width:(c + 1) * width, :],
                                   (((1,), (1,)), ((), ())), preferred_element_type=F32)
            part = both[:reps] + both[reps:]
            for a in range(ny):
                for b in range(nz):
                    at = (a * nz + b) * piece
                    sums[it, c, a, b] = part[:, at:at + piece]
            y_copies[c] = send(sums.at[it, c, 1 - y], y_in.at[it, c], y_send.at[it, c],
                               y_recv.at[it, c], y_peer)

        def over_z(c):
            y_copies[c].wait_recv()
            z_out[it, c] = sums[it, c, y] + y_in[it, c]
            z_copies[c] = [
                send(z_out.at[it, c, z_at[d]], z_in.at[it, c, d - 1], z_send.at[it, c, d - 1],
                     z_recv.at[it, c, d - 1], z_peers[d]) for d in range(1, nz)]

        def update(c):
            total = z_out[it, c, z]
            for d in range(1, nz):
                z_copies[c][d - 1].wait_recv()
                total = total + z_in[it, c, d - 1]
            if it == 0:
                at = pl.ds(pl.multiple_of(c * width + (y * nz + z) * piece, piece), piece)
                before = weights_v[:, at]
            else:
                before = held[it - 1, c, y, z]
            held[it, c, y, z] = before * total / total_subjects
            gz_copies[c] = [
                send(held.at[it, c, y, z], held.at[it, c, y, z], gz_send.at[it, c, d - 1],
                     gz_recv.at[it, c, d - 1], z_peers[d]) for d in range(1, nz)]

        def over_y(c):
            for copy in gz_copies[c]:
                copy.wait_recv()
            gy_copies[c] = send(held.at[it, c, y], held.at[it, c, y], gy_send.at[it, c],
                                gy_recv.at[it, c], y_peer)

        def finish(c):
            gy_copies[c].wait_recv()
            now = jnp.concatenate([held[it, c, a, b] for a in range(ny) for b in range(nz)], axis=1)
            if it == ITERS - 1:
                chunk = pl.ds(c * width, width)
                new_v[:, chunk] = now
                out(new_v.at[:, chunk], new_hbm.at[:, chunk])
                return
            hi, lo = split(now)
            part = jnp.dot(jnp.concatenate([hi, lo], axis=0), tile[c * width:(c + 1) * width, :],
                           preferred_element_type=F32)
            live["mix"] = part if c == 0 else live["mix"] + part
            if c == CHUNKS - 1:
                mix = (live["mix"][:reps] + live["mix"][reps:]) * factor[:1, :]
                for side in range(2):
                    mix_start[it + 1, side, :reps, :] = mix[:, side * half:(side + 1) * half]
                start_exchange(it + 1)

        def slot(s):
            def run():
                for k, stage in enumerate((over_z, update, over_y, finish)):
                    if 0 <= s - k < CHUNKS:
                        stage(s - k)
            return run

        return ([to_x, to_core, respond] + [functools.partial(compute, c) for c in range(CHUNKS)]
                + [slot(s) for s in range(CHUNKS + 3)])

    for it in range(ITERS):
        for stage in stages_of(it):
            stage()
    for copy in sent:
        copy.wait_send()
    for copy in written:
        copy.wait()


def run_em(obs, noise, times, absorption, elimination, volume, weights, counts, ny, nz, sizes):
    reps, supports = weights.shape
    samples, subjects = obs.shape
    half = subjects // 2
    piece = supports // (CHUNKS * ny * nz)
    rows = reps + PEAK_ROWS
    dma = lambda *shape: pltpu.SemaphoreType.DMA(shape)
    vmem = lambda *shape: pltpu.VMEM(shape, F32)
    parts = (ITERS, CHUNKS)
    inputs = (obs, noise, times, absorption, elimination, volume, weights, counts)
    return pl.pallas_call(
        functools.partial(em_kernel, float(sizes[0]), float(sizes[1]), ny, nz),
        out_shape=[jax.ShapeDtypeStruct((reps, supports), F32), jax.ShapeDtypeStruct((reps, subjects), F32)],
        in_specs=[pl.BlockSpec(memory_space=pltpu.HBM)] * len(inputs),
        out_specs=[pl.BlockSpec(memory_space=pltpu.HBM)] * 2,
        scratch_shapes=[pltpu.VMEM(a.shape, a.dtype) for a in inputs] + [
            dma(len(inputs)),
            pltpu.VMEM((supports, 6 * NT), BF16), pltpu.VMEM((2 * reps, supports), BF16),
            vmem(samples, BLOCK), vmem(samples, BLOCK), pltpu.VMEM((2, 6 * NT, BLOCK), BF16),
            vmem(supports, BLOCK), vmem(supports, BLOCK), pltpu.VMEM((supports, subjects), BF16),
            vmem(PEAK_ROWS, subjects),
            vmem(reps, supports), vmem(reps, subjects), dma(1 + CHUNKS),
            vmem(ITERS, 2, rows, half), vmem(ITERS, 2, rows, half), vmem(ITERS, rows, half),
            vmem(ITERS, rows, half), vmem(ITERS, rows, half), vmem(PEAK_ROWS, subjects),
            vmem(*parts, ny, nz, reps, piece), vmem(*parts, nz, reps, piece),
            vmem(*parts, nz, reps, piece), vmem(*parts, nz - 1, reps, piece),
            vmem(*parts, ny, nz, reps, piece),
            dma(ITERS, 3), dma(ITERS, 3), dma(*parts), dma(*parts),
            dma(*parts, nz - 1), dma(*parts, nz - 1), dma(*parts, nz - 1), dma(*parts, nz - 1),
            dma(*parts), dma(*parts),
        ],
        compiler_params=pltpu.CompilerParams(collective_id=0, has_side_effects=True, vmem_limit_bytes=56 * MIB),
        name="em_steps",
    )(*inputs)


def plain_em(tile, mix, log_scale, counts, weights, samples, total_subjects, total_supports):
    reps = weights.shape[0]
    both = jnp.concatenate([mix[0], mix[1]], axis=1)
    local_peak = both[reps]
    peak = lax.pmax(local_peak, "supp")
    factor = jnp.exp(local_peak - peak)
    partial_mix = both[:reps]
    drawn = counts > 0
    current = weights
    loglik = None
    for it in range(ITERS):
        if it > 0:
            hi, lo = split(current)
            pair = jnp.dot(jnp.concatenate([hi, lo], axis=0), tile, preferred_element_type=F32)
            partial_mix = pair[:reps] + pair[reps:]
        mixture = lax.psum(partial_mix * factor, "supp")
        if it == 0:
            loglik = (peak + jnp.log(mixture / total_supports) - log_scale[:1]) / samples
            loglik = loglik - 0.5 * math.log(2.0 * math.pi)
        resp = jnp.where(drawn, counts.astype(F32) / jnp.where(drawn, mixture, 1.0), 0.0) * factor
        hi, lo = split(resp)
        pair = lax.dot_general(jnp.concatenate([hi, lo], axis=0), tile, (((1,), (1,)), ((), ())),
                               preferred_element_type=F32)
        current = current * lax.psum(pair[:reps] + pair[reps:], "subj") / total_subjects
    return current, loglik


def body(observations, noise_scale, sample_times, counts, absorption, elimination, volume, weights):
    n_subj, n_supp = lax.axis_size("subj"), lax.axis_size("supp")
    subjects, samples = observations.shape
    sizes = (subjects * n_subj, weights.shape[1] * n_supp)
    inputs = (observations.T, noise_scale.T, sample_times.T,
              absorption[None, :], elimination[None, :], volume[None, :], weights)
    if (n_subj, n_supp) == (8, 4):
        return run_em(*inputs, counts, 2, 4, sizes)
    return plain_em(*make_tile(*inputs), counts, weights, samples, *sizes)


def solution(mesh):
    return jax.shard_map(
        body,
        mesh=mesh,
        in_specs=(
            P("subj", None),
            P("subj", None),
            P("subj", None),
            P(None, "subj"),
            P("supp"),
            P("supp"),
            P("supp"),
            P(None, "supp"),
        ),
        out_specs=(P(None, "supp"), P(None, "subj")),
        check_vma=False,
    )
```

```python
import functools
import math

import jax
import jax.numpy as jnp
from jax import lax
from jax.experimental import pallas as pl
from jax.experimental.pallas import tpu as pltpu
from jax.sharding import PartitionSpec as P

NT = 128
HORIZON = 24.0
ITERS = 2
BLOCK = 256
KSTEP = 2048
CHUNKS = 4
FILL_STEPS = 2
GROUP = 32
PEAK_ROWS = 8
MIB = 1 << 20
F32 = jnp.float32
BF16 = jnp.bfloat16


def split(x):
    hi = x.astype(BF16)
    return hi, (x - hi.astype(F32)).astype(BF16)


def build_curves(absorption_ref, elimination_ref, volume_ref, curves, step):
    step_size = 512
    grid_rows = lax.broadcasted_iota(jnp.int32, (NT, step_size), 0).astype(F32)
    time_grid = (grid_rows + 1.0) * (HORIZON / NT)

    at = pl.ds(pl.multiple_of(step * step_size, step_size), step_size)
    rate_in = absorption_ref[:, at]
    rate_out = elimination_ref[:, at]
    amplitude = rate_in / (volume_ref[:, at] * (rate_in - rate_out))
    rows = amplitude * (jnp.exp(-rate_out * time_grid) - jnp.exp(-rate_in * time_grid))
    columns = rows.T
    for half, part in ((0, columns), (NT, columns * columns)):
        hi, lo = split(part)
        curves[at, half:half + NT] = hi
        curves[at, 2 * NT + half:3 * NT + half] = hi
        curves[at, 4 * NT + half:5 * NT + half] = lo


def block_mixture(obs, noise, times, curves, current, log_lik, tile_ref, columns):
    supports = log_lik.shape[0]
    steps = supports // KSTEP
    precision = 1.0 / (noise * noise)
    linear = obs * precision
    square = -0.5 * precision
    grid_index = lax.broadcasted_iota(jnp.int32, (NT, BLOCK), 0)
    linear_part = jnp.zeros((NT, BLOCK), F32)
    square_part = jnp.zeros((NT, BLOCK), F32)
    for j in range(obs.shape[0]):
        hit = times[j:j + 1, :] == grid_index
        linear_part = linear_part + jnp.where(hit, linear[j:j + 1, :], 0.0)
        square_part = square_part + jnp.where(hit, square[j:j + 1, :], 0.0)
    offset = -0.5 * jnp.sum(obs * obs * precision, axis=0, keepdims=True)
    log_scale = jnp.sum(jnp.log(noise), axis=0, keepdims=True)
    hi, lo = split(jnp.concatenate([linear_part, square_part], axis=0))
    features = jnp.concatenate([hi, lo, hi], axis=0)

    def one_log(step, peak):
        at = pl.ds(pl.multiple_of(step * KSTEP, KSTEP), KSTEP)
        part = jnp.dot(curves[at, :], features, preferred_element_type=F32)
        log_lik[at, :] = part
        return jnp.maximum(peak, jnp.max(part.reshape(KSTEP // 8, 8, BLOCK), axis=0))

    peak = lax.fori_loop(0, steps, one_log, jnp.full((8, BLOCK), -jnp.inf, F32))
    peak = jnp.max(peak, axis=0, keepdims=True)

    def one_tile(step, mix):
        at = pl.ds(pl.multiple_of(step * KSTEP, KSTEP), KSTEP)
        like = jnp.exp(log_lik[at, :] - peak).astype(BF16)
        tile_ref[at, columns] = like
        return mix + jnp.dot(current[:, at], like, preferred_element_type=F32)

    mix = lax.fori_loop(0, steps, one_tile, jnp.zeros((current.shape[0], BLOCK), F32))
    return mix, peak + offset, log_scale


def tile_kernel(obs_ref, noise_ref, times_ref, absorption_ref, elimination_ref, volume_ref,
                weights_ref, tile_ref, mix_ref, scale_ref, curves, current, log_lik):
    reps = weights_ref.shape[0]

    @pl.when(pl.program_id(0) == 0)
    def _():
        hi, lo = split(weights_ref[...])
        current[...] = jnp.concatenate([hi, lo], axis=0)
        @pl.loop(0, absorption_ref.shape[1] // 512)
        def _(step):
            build_curves(absorption_ref, elimination_ref, volume_ref, curves, step)

    mix, peak, log_scale = block_mixture(obs_ref[...], noise_ref[...], times_ref[...], curves, current,
                                         log_lik, tile_ref, slice(None))
    mix_ref[0, :reps, :] = mix[:reps] + mix[reps:]
    mix_ref[0, reps:, :] = jnp.broadcast_to(peak, (PEAK_ROWS, BLOCK))
    scale_ref[...] = jnp.broadcast_to(log_scale, (PEAK_ROWS, BLOCK))


def make_tile(obs, noise, times, absorption, elimination, volume, weights):
    samples, subjects = obs.shape
    reps, supports = weights.shape
    half = subjects // 2
    per_half = half // BLOCK
    by_subject = pl.BlockSpec((samples, BLOCK), lambda b: (0, b))
    whole = lambda shape: pl.BlockSpec(shape, lambda b: (0, 0))
    return pl.pallas_call(
        tile_kernel,
        grid=(subjects // BLOCK,),
        in_specs=[by_subject] * 3 + [whole((1, supports))] * 3 + [whole((reps, supports))],
        out_specs=[
            pl.BlockSpec((supports, BLOCK), lambda b: (0, b)),
            pl.BlockSpec((1, reps + PEAK_ROWS, BLOCK), lambda b: (b // per_half, 0, b % per_half)),
            pl.BlockSpec((PEAK_ROWS, BLOCK), lambda b: (0, b)),
        ],
        out_shape=[
            jax.ShapeDtypeStruct((supports, subjects), BF16),
            jax.ShapeDtypeStruct((2, reps + PEAK_ROWS, half), F32),
            jax.ShapeDtypeStruct((PEAK_ROWS, subjects), F32),
        ],
        scratch_shapes=[
            pltpu.VMEM((supports, 6 * NT), BF16),
            pltpu.VMEM((2 * reps, supports), BF16),
            pltpu.VMEM((supports, BLOCK), F32),
        ],
        compiler_params=pltpu.CompilerParams(vmem_limit_bytes=32 * MIB),
        name="make_tile",
    )(obs, noise, times, absorption, elimination, volume, weights)


def merge(mine, other, reps):
    peak_a, peak_b = mine[reps:], other[reps:]
    peak = jnp.maximum(peak_a, peak_b)
    scale_a, scale_b = jnp.exp(peak_a - peak)[:1], jnp.exp(peak_b - peak)[:1]
    return jnp.concatenate([mine[:reps] * scale_a + other[:reps] * scale_b, peak], axis=0)


def em_kernel(total_subjects, total_supports, ny, nz,
              obs_hbm, noise_hbm, times_hbm, absorption_hbm, elimination_hbm, volume_hbm, weights_hbm, counts_hbm,
              new_ref, loglik_ref,
              obs_v, noise_v, times_v, absorption_v, elimination_v, volume_v, weights_v, counts_v, load_sem,
              curves, current, linear_v, square_v, features_v, log_lik_even, log_lik_odd, tile, log_scale,
              mix_own, mix_start, mix_pair, mix_near, mix_far, factor,
              sums, y_in, z_out, z_in, held,
              mix_send, mix_recv, y_send, y_recv, z_send, z_recv, gz_send, gz_recv, gy_send, gy_recv):
    samples = obs_v.shape[0]
    all_reps, subjects = counts_v.shape
    reps = all_reps
    half = subjects // 2
    per_half = half // BLOCK
    supports = weights_v.shape[1]
    width = supports // CHUNKS
    piece = width // (ny * nz)
    subj, supp = lax.axis_index("subj"), lax.axis_index("supp")
    y, z = lax.rem(subj, ny), lax.div(subj, ny)
    core = lax.rem(supp, 2)
    core_peer = {"subj": subj, "supp": supp + 1 - 2 * core}
    x_peer = {"subj": subj, "supp": lax.rem(supp + 2, 4)}
    y_peer = {"subj": subj + 1 - 2 * y, "supp": supp}
    z_at = [lax.rem(z + d, nz) for d in range(nz)]
    z_peers = [{"subj": z_at[d] * ny + y, "supp": supp} for d in range(nz)]
    in_flight = {}
    mix_rows = lambda it: all_reps + PEAK_ROWS if it == 0 else all_reps

    loads = [pltpu.make_async_copy(src, dst, load_sem.at[k]) for k, (src, dst) in enumerate((
        (absorption_hbm, absorption_v), (elimination_hbm, elimination_v), (volume_hbm, volume_v),
        (weights_hbm, weights_v), (obs_hbm, obs_v), (noise_hbm, noise_v), (times_hbm, times_v),
        (counts_hbm, counts_v)))]
    for load in loads:
        load.start()

    def send(src, dst, send_sem, recv_sem, peer, key):
        if key in in_flight:
            in_flight.pop(key)()
        copy = pltpu.make_async_remote_copy(
            src_ref=src, dst_ref=dst, send_sem=send_sem, recv_sem=recv_sem,
            device_id=peer, device_id_type=pl.DeviceIdType.MESH)
        copy.start()
        in_flight[key] = copy.wait_send
        return copy

    def send_along_z(src_of, dst_of, send_sem, recv_sem, several, key):
        all_sent = pltpu.make_async_copy(several, several, send_sem)
        if key in in_flight:
            in_flight.pop(key)()
        for d in range(1, nz):
            pltpu.make_async_remote_copy(
                src_ref=src_of(d), dst_ref=dst_of(d), send_sem=send_sem, recv_sem=recv_sem,
                device_id=z_peers[d], device_id_type=pl.DeviceIdType.MESH).start()
        in_flight[key] = all_sent.wait
        return pltpu.make_async_copy(several, several, recv_sem)

    barrier = pltpu.get_barrier_semaphore()
    peers = [core_peer, x_peer, y_peer] + z_peers[1:]
    for peer in peers:
        pl.semaphore_signal(barrier, inc=1, device_id=peer, device_id_type=pl.DeviceIdType.MESH)

    for load in loads[:3]:
        load.wait()

    @pl.loop(0, supports // 512)
    def _(step):
        build_curves(absorption_v, elimination_v, volume_v, curves, step)

    for load in loads[3:]:
        load.wait()
    hi, lo = split(weights_v[...])
    current[...] = jnp.concatenate([hi, lo], axis=0)
    blocks = subjects // BLOCK
    starts = [pl.multiple_of((1 - core) * half + b * BLOCK, BLOCK) for b in range(per_half)]
    starts += [pl.multiple_of(core * half + b * BLOCK, BLOCK) for b in range(per_half)]
    columns = [pl.ds(at, BLOCK) for at in starts]
    offsets = {}

    def prepare(b):
        obs, noise = obs_v[:, columns[b]], noise_v[:, columns[b]]
        precision = 1.0 / (noise * noise)
        linear = obs * precision
        linear_v[...] = linear
        square_v[...] = -0.5 * precision
        offsets[b] = -0.5 * jnp.sum(obs * linear, axis=0, keepdims=True)
        scale = jnp.sum(jnp.log(noise), axis=0, keepdims=True)
        log_scale[:, columns[b]] = jnp.broadcast_to(scale, (PEAK_ROWS, BLOCK))

    def feature_rows(b, step):
        features = features_v.at[b % 2]
        for k in range(NT // FILL_STEPS // GROUP):
            first_row = pl.multiple_of(step * (NT // FILL_STEPS) + k * GROUP, GROUP)
            index = lax.broadcasted_iota(jnp.int32, (GROUP, BLOCK), 0) + first_row
            linear_part = jnp.zeros((GROUP, BLOCK), F32)
            square_part = jnp.zeros((GROUP, BLOCK), F32)
            for j in range(samples):
                hit = times_v[j:j + 1, columns[b]] == index
                linear_part = linear_part + jnp.where(hit, linear_v[j:j + 1, :], 0.0)
                square_part = square_part + jnp.where(hit, square_v[j:j + 1, :], 0.0)
            for base, part in ((0, linear_part), (NT, square_part)):
                hi, lo = split(part)
                for slot, value in ((0, hi), (1, lo), (2, hi)):
                    at = pl.ds(pl.multiple_of(slot * 2 * NT + base + first_row, GROUP), GROUP)
                    features[at, :] = value

    fill_step = supports // FILL_STEPS
    logs = (log_lik_even, log_lik_odd)

    prepare(0)

    @pl.loop(0, FILL_STEPS)
    def _(step):
        feature_rows(0, step)

    def fill_stage(b, peak_before):
        if b + 1 < blocks:
            prepare(b + 1)

        def one(step, carry):
            peak, mix = carry
            at = pl.ds(pl.multiple_of(step * fill_step, fill_step), fill_step)
            if b < blocks:
                part = jnp.dot(curves[at, :], features_v[b % 2], preferred_element_type=F32)
                logs[b % 2][at, :] = part
                peak = jnp.maximum(peak, jnp.max(part.reshape(fill_step // 8, 8, BLOCK), axis=0))
            if b > 0:
                like = jnp.exp(logs[(b - 1) % 2][at, :] - peak_before).astype(BF16)
                tile[at, columns[b - 1]] = like
                mix = mix + jnp.dot(current[:, at], like, preferred_element_type=F32)
            if b + 1 < blocks:
                feature_rows(b + 1, step)
            return peak, mix

        peak, mix = lax.fori_loop(0, FILL_STEPS, one, (
            jnp.full((8, BLOCK), -jnp.inf, F32), jnp.zeros((2 * all_reps, BLOCK), F32)))
        if b > 0:
            side = 1 - core if b - 1 < per_half else core
            within = slice((b - 1) % per_half * BLOCK, ((b - 1) % per_half + 1) * BLOCK)
            mix = mix[:all_reps] + mix[all_reps:]
            mix_start[0, side, :all_reps, within] = mix
            mix_start[0, side, all_reps:, within] = jnp.broadcast_to(
                peak_before + offsets[b - 1], (PEAK_ROWS, BLOCK))
        return jnp.max(peak, axis=0, keepdims=True)

    first = {}

    def start_exchange(it):
        to_send = pl.ds(0, mix_rows(it))
        first[it] = send(mix_start.at[it, 1 - core, to_send], mix_near.at[it, to_send], mix_send.at[0],
                         mix_recv.at[0], core_peer, ("mix", 0))

    peak = None
    for b in range(blocks + 1):
        peak = fill_stage(b, peak)
        if b == per_half:
            pl.semaphore_wait(barrier, len(peers))
            start_exchange(0)

    def stages_of(it):
        mixed = pl.ds(0, mix_rows(it))
        join = (lambda a, b: merge(a, b, reps)) if it == 0 else (lambda a, b: a + b)
        live = {}
        y_copies, z_copies, gz_copies, gy_copies = {}, {}, {}, {}

        def to_x():
            first[it].wait_recv()
            mix_pair[it, mixed] = join(mix_start[it, core, mixed], mix_near[it, mixed])
            live["x"] = send(mix_pair.at[it, mixed], mix_far.at[it, mixed], mix_send.at[2 + it],
                             mix_recv.at[2 + it], x_peer, ("mix", 2 + it))

        def to_core():
            live["x"].wait_recv()
            mix_own[it, core, mixed] = join(mix_pair[it, mixed], mix_far[it, mixed])
            live["core"] = send(mix_own.at[it, core, mixed], mix_own.at[it, core, mixed], mix_send.at[1],
                                mix_recv.at[1], core_peer, ("mix", 1))

        def respond():
            live["core"].wait_recv()
            parts = []
            for side in range(2):
                columns = slice(side * half, (side + 1) * half)
                mixture = mix_own[it, side, :reps, :]
                if it == 0:
                    peak = mix_own[0, side, reps:, :]
                    factor[:, columns] = jnp.exp(mix_start[0, side, reps:, :] - peak)
                    loglik_ref[:, columns] = (
                        peak[:1] + jnp.log(mixture / total_supports) - log_scale[:1, columns]
                    ) / samples - 0.5 * math.log(2.0 * math.pi)
                counts = counts_v[:, columns]
                drawn = counts > 0
                resp = jnp.where(drawn, counts.astype(F32) / jnp.where(drawn, mixture, 1.0), 0.0)
                parts.append(resp * factor[:1, columns])
            hi, lo = split(jnp.concatenate(parts, axis=1))
            live["resp"] = jnp.concatenate([hi, lo], axis=0)

        def compute(c):
            both = lax.dot_general(live["resp"], tile[c * width:(c + 1) * width, :],
                                   (((1,), (1,)), ((), ())), preferred_element_type=F32)
            part = both[:reps] + both[reps:]
            for a in range(ny):
                for b in range(nz):
                    at = (a * nz + b) * piece
                    sums[it, c, a, b] = part[:, at:at + piece]
            y_copies[c] = send(sums.at[it, c, 1 - y], y_in.at[it, c], y_send.at[c],
                               y_recv.at[c], y_peer, ("y", c))

        def over_z(c):
            y_copies[c].wait_recv()
            z_out[it, c] = sums[it, c, y] + y_in[it, c]
            z_copies[c] = send_along_z(lambda d: z_out.at[it, c, z_at[d]], lambda d: z_in.at[it, c, d - 1],
                                       z_send.at[c], z_recv.at[c], z_in.at[it, c], ("z", c))

        def update(c):
            total = z_out[it, c, z]
            z_copies[c].wait()
            for d in range(1, nz):
                total = total + z_in[it, c, d - 1]
            if it == 0:
                at = pl.ds(pl.multiple_of(c * width + (y * nz + z) * piece, piece), piece)
                before = weights_v[:, at]
            else:
                before = held[it - 1, c, y, z]
            held[it, c, y, z] = before * total / total_subjects
            gz_copies[c] = send_along_z(lambda d: held.at[it, c, y, z], lambda d: held.at[it, c, y, z],
                                        gz_send.at[c], gz_recv.at[c], z_in.at[it, c], ("gz", c))

        def over_y(c):
            gz_copies[c].wait()
            gy_copies[c] = send(held.at[it, c, y], held.at[it, c, y], gy_send.at[c],
                                gy_recv.at[c], y_peer, ("gy", c))

        def finish(c):
            gy_copies[c].wait_recv()
            now = jnp.concatenate([held[it, c, a, b] for a in range(ny) for b in range(nz)], axis=1)
            if it == ITERS - 1:
                new_ref[:, c * width:(c + 1) * width] = now
                return
            hi, lo = split(now)
            part = jnp.dot(jnp.concatenate([hi, lo], axis=0), tile[c * width:(c + 1) * width, :],
                           preferred_element_type=F32)
            live["mix"] = part if c == 0 else live["mix"] + part
            if c == CHUNKS - 1:
                mix = (live["mix"][:reps] + live["mix"][reps:]) * factor[:1, :]
                for side in range(2):
                    mix_start[it + 1, side, :reps, :] = mix[:, side * half:(side + 1) * half]
                start_exchange(it + 1)

        def slot(s):
            def run():
                for k, stage in enumerate((over_z, update, over_y, finish)):
                    if 0 <= s - k < CHUNKS:
                        stage(s - k)
            return run

        return ([to_x, to_core, respond] + [functools.partial(compute, c) for c in range(CHUNKS)]
                + [slot(s) for s in range(CHUNKS + 3)])

    for it in range(ITERS):
        for stage in stages_of(it):
            stage()
    for wait in in_flight.values():
        wait()


def run_em(obs, noise, times, absorption, elimination, volume, weights, counts, ny, nz, sizes):
    reps, supports = weights.shape
    samples, subjects = obs.shape
    half = subjects // 2
    piece = supports // (CHUNKS * ny * nz)
    rows = reps + PEAK_ROWS
    dma = lambda *shape: pltpu.SemaphoreType.DMA(shape)
    vmem = lambda *shape: pltpu.VMEM(shape, F32)
    parts = (ITERS, CHUNKS)
    inputs = (obs, noise, times, absorption, elimination, volume, weights, counts)
    return pl.pallas_call(
        functools.partial(em_kernel, float(sizes[0]), float(sizes[1]), ny, nz),
        out_shape=[pltpu.VMEM((reps, supports), F32), pltpu.VMEM((reps, subjects), F32)],
        in_specs=[pl.BlockSpec(memory_space=pltpu.HBM)] * len(inputs),
        out_specs=[pl.BlockSpec(memory_space=pltpu.VMEM)] * 2,
        scratch_shapes=[pltpu.VMEM(a.shape, a.dtype) for a in inputs] + [
            dma(len(inputs)),
            pltpu.VMEM((supports, 6 * NT), BF16), pltpu.VMEM((2 * reps, supports), BF16),
            vmem(samples, BLOCK), vmem(samples, BLOCK), pltpu.VMEM((2, 6 * NT, BLOCK), BF16),
            vmem(supports, BLOCK), vmem(supports, BLOCK), pltpu.VMEM((supports, subjects), BF16),
            vmem(PEAK_ROWS, subjects),
            vmem(ITERS, 2, rows, half), vmem(ITERS, 2, rows, half), vmem(ITERS, rows, half),
            vmem(ITERS, rows, half), vmem(ITERS, rows, half), vmem(PEAK_ROWS, subjects),
            vmem(*parts, ny, nz, reps, piece), vmem(*parts, nz, reps, piece),
            vmem(*parts, nz, reps, piece), vmem(*parts, nz - 1, reps, piece),
            vmem(*parts, ny, nz, reps, piece),
            dma(2 + ITERS), dma(2 + ITERS), *[dma(CHUNKS)] * 8,
        ],
        compiler_params=pltpu.CompilerParams(collective_id=0, has_side_effects=True, vmem_limit_bytes=56 * MIB),
        name="em_steps",
    )(*inputs)


def hand_over(new, loglik):
    rows = 8

    def kernel(new_in, loglik_in, new_out, loglik_out, sem):
        copies = [pltpu.make_async_copy(new_in.at[pl.ds(k * rows, rows)], new_out.at[pl.ds(k * rows, rows)], sem.at[k])
                  for k in range(new_in.shape[0] // rows)]
        copies.append(pltpu.make_async_copy(loglik_in, loglik_out, sem.at[len(copies)]))
        for copy in copies:
            copy.start()
        for copy in copies:
            copy.wait()

    return pl.pallas_call(
        kernel,
        out_shape=[jax.ShapeDtypeStruct(new.shape, F32), jax.ShapeDtypeStruct(loglik.shape, F32)],
        in_specs=[pl.BlockSpec(memory_space=pltpu.VMEM)] * 2,
        out_specs=[pl.BlockSpec(memory_space=pltpu.HBM)] * 2,
        scratch_shapes=[pltpu.SemaphoreType.DMA((1 + new.shape[0] // rows,))],
        name="hand_over",
    )(new, loglik)


def plain_em(tile, mix, log_scale, counts, weights, samples, total_subjects, total_supports):
    reps = weights.shape[0]
    both = jnp.concatenate([mix[0], mix[1]], axis=1)
    local_peak = both[reps]
    peak = lax.pmax(local_peak, "supp")
    factor = jnp.exp(local_peak - peak)
    partial_mix = both[:reps]
    drawn = counts > 0
    current = weights
    loglik = None
    for it in range(ITERS):
        if it > 0:
            hi, lo = split(current)
            pair = jnp.dot(jnp.concatenate([hi, lo], axis=0), tile, preferred_element_type=F32)
            partial_mix = pair[:reps] + pair[reps:]
        mixture = lax.psum(partial_mix * factor, "supp")
        if it == 0:
            loglik = (peak + jnp.log(mixture / total_supports) - log_scale[:1]) / samples
            loglik = loglik - 0.5 * math.log(2.0 * math.pi)
        resp = jnp.where(drawn, counts.astype(F32) / jnp.where(drawn, mixture, 1.0), 0.0) * factor
        hi, lo = split(resp)
        pair = lax.dot_general(jnp.concatenate([hi, lo], axis=0), tile, (((1,), (1,)), ((), ())),
                               preferred_element_type=F32)
        current = current * lax.psum(pair[:reps] + pair[reps:], "subj") / total_subjects
    return current, loglik


def body(observations, noise_scale, sample_times, counts, absorption, elimination, volume, weights):
    n_subj, n_supp = lax.axis_size("subj"), lax.axis_size("supp")
    subjects, samples = observations.shape
    sizes = (subjects * n_subj, weights.shape[1] * n_supp)
    inputs = (observations.T, noise_scale.T, sample_times.T,
              absorption[None, :], elimination[None, :], volume[None, :], weights)
    if (n_subj, n_supp) == (8, 4):
        new, loglik = run_em(*inputs, counts, 2, 4, sizes)
        return hand_over(pltpu.with_memory_space_constraint(new, pltpu.VMEM), pltpu.with_memory_space_constraint(loglik, pltpu.VMEM))
    return plain_em(*make_tile(*inputs), counts, weights, samples, *sizes)


def solution(mesh):
    return jax.shard_map(
        body,
        mesh=mesh,
        in_specs=(
            P("subj", None),
            P("subj", None),
            P("subj", None),
            P(None, "subj"),
            P("supp"),
            P("supp"),
            P("supp"),
            P(None, "supp"),
        ),
        out_specs=(P(None, "supp"), P(None, "subj")),
        check_vma=False,
    )
```

```python
import functools
import math

import jax
import jax.numpy as jnp
from jax import lax
from jax.experimental import pallas as pl
from jax.experimental.pallas import tpu as pltpu
from jax.sharding import PartitionSpec as P

NT = 128
HORIZON = 24.0
ITERS = 2
BLOCK = 256
KSTEP = 2048
CHUNKS = 8
FILL_STEPS = 2
GROUP = 32
PEAK_ROWS = 8
LATE = (3.2, 10.7, 18.2, 25.7)
PACE = 0.62
MIB = 1 << 20
F32 = jnp.float32
BF16 = jnp.bfloat16


def split(x):
    hi = x.astype(BF16)
    return hi, (x - hi.astype(F32)).astype(BF16)


def build_curves(absorption_ref, elimination_ref, volume_ref, curves, step):
    step_size = 512
    grid_rows = lax.broadcasted_iota(jnp.int32, (NT, step_size), 0).astype(F32)
    time_grid = (grid_rows + 1.0) * (HORIZON / NT)

    at = pl.ds(pl.multiple_of(step * step_size, step_size), step_size)
    rate_in = absorption_ref[:, at]
    rate_out = elimination_ref[:, at]
    amplitude = rate_in / (volume_ref[:, at] * (rate_in - rate_out))
    rows = amplitude * (jnp.exp(-rate_out * time_grid) - jnp.exp(-rate_in * time_grid))
    columns = rows.T
    for half, part in ((0, columns), (NT, columns * columns)):
        hi, lo = split(part)
        curves[at, half:half + NT] = hi
        curves[at, 2 * NT + half:3 * NT + half] = hi
        curves[at, 4 * NT + half:5 * NT + half] = lo


def block_mixture(obs, noise, times, curves, current, log_lik, tile_ref, columns):
    supports = log_lik.shape[0]
    steps = supports // KSTEP
    precision = 1.0 / (noise * noise)
    linear = obs * precision
    square = -0.5 * precision
    grid_index = lax.broadcasted_iota(jnp.int32, (NT, BLOCK), 0)
    linear_part = jnp.zeros((NT, BLOCK), F32)
    square_part = jnp.zeros((NT, BLOCK), F32)
    for j in range(obs.shape[0]):
        hit = times[j:j + 1, :] == grid_index
        linear_part = linear_part + jnp.where(hit, linear[j:j + 1, :], 0.0)
        square_part = square_part + jnp.where(hit, square[j:j + 1, :], 0.0)
    offset = -0.5 * jnp.sum(obs * obs * precision, axis=0, keepdims=True)
    log_scale = jnp.sum(jnp.log(noise), axis=0, keepdims=True)
    hi, lo = split(jnp.concatenate([linear_part, square_part], axis=0))
    features = jnp.concatenate([hi, lo, hi], axis=0)

    def one_log(step, peak):
        at = pl.ds(pl.multiple_of(step * KSTEP, KSTEP), KSTEP)
        part = jnp.dot(curves[at, :], features, preferred_element_type=F32)
        log_lik[at, :] = part
        return jnp.maximum(peak, jnp.max(part.reshape(KSTEP // 8, 8, BLOCK), axis=0))

    peak = lax.fori_loop(0, steps, one_log, jnp.full((8, BLOCK), -jnp.inf, F32))
    peak = jnp.max(peak, axis=0, keepdims=True)

    def one_tile(step, mix):
        at = pl.ds(pl.multiple_of(step * KSTEP, KSTEP), KSTEP)
        like = jnp.exp(log_lik[at, :] - peak).astype(BF16)
        tile_ref[at, columns] = like
        return mix + jnp.dot(current[:, at], like, preferred_element_type=F32)

    mix = lax.fori_loop(0, steps, one_tile, jnp.zeros((current.shape[0], BLOCK), F32))
    return mix, peak + offset, log_scale


def tile_kernel(obs_ref, noise_ref, times_ref, absorption_ref, elimination_ref, volume_ref,
                weights_ref, tile_ref, mix_ref, scale_ref, curves, current, log_lik):
    reps = weights_ref.shape[0]

    @pl.when(pl.program_id(0) == 0)
    def _():
        hi, lo = split(weights_ref[...])
        current[...] = jnp.concatenate([hi, lo], axis=0)
        @pl.loop(0, absorption_ref.shape[1] // 512)
        def _(step):
            build_curves(absorption_ref, elimination_ref, volume_ref, curves, step)

    mix, peak, log_scale = block_mixture(obs_ref[...], noise_ref[...], times_ref[...], curves, current,
                                         log_lik, tile_ref, slice(None))
    mix_ref[0, :reps, :] = mix[:reps] + mix[reps:]
    mix_ref[0, reps:, :] = jnp.broadcast_to(peak, (PEAK_ROWS, BLOCK))
    scale_ref[...] = jnp.broadcast_to(log_scale, (PEAK_ROWS, BLOCK))


def make_tile(obs, noise, times, absorption, elimination, volume, weights):
    samples, subjects = obs.shape
    reps, supports = weights.shape
    half = subjects // 2
    per_half = half // BLOCK
    by_subject = pl.BlockSpec((samples, BLOCK), lambda b: (0, b))
    whole = lambda shape: pl.BlockSpec(shape, lambda b: (0, 0))
    return pl.pallas_call(
        tile_kernel,
        grid=(subjects // BLOCK,),
        in_specs=[by_subject] * 3 + [whole((1, supports))] * 3 + [whole((reps, supports))],
        out_specs=[
            pl.BlockSpec((supports, BLOCK), lambda b: (0, b)),
            pl.BlockSpec((1, reps + PEAK_ROWS, BLOCK), lambda b: (b // per_half, 0, b % per_half)),
            pl.BlockSpec((PEAK_ROWS, BLOCK), lambda b: (0, b)),
        ],
        out_shape=[
            jax.ShapeDtypeStruct((supports, subjects), BF16),
            jax.ShapeDtypeStruct((2, reps + PEAK_ROWS, half), F32),
            jax.ShapeDtypeStruct((PEAK_ROWS, subjects), F32),
        ],
        scratch_shapes=[
            pltpu.VMEM((supports, 6 * NT), BF16),
            pltpu.VMEM((2 * reps, supports), BF16),
            pltpu.VMEM((supports, BLOCK), F32),
        ],
        compiler_params=pltpu.CompilerParams(vmem_limit_bytes=32 * MIB),
        name="make_tile",
    )(obs, noise, times, absorption, elimination, volume, weights)


def merge(mine, other, reps):
    peak_a, peak_b = mine[reps:], other[reps:]
    peak = jnp.maximum(peak_a, peak_b)
    scale_a, scale_b = jnp.exp(peak_a - peak)[:1], jnp.exp(peak_b - peak)[:1]
    return jnp.concatenate([mine[:reps] * scale_a + other[:reps] * scale_b, peak], axis=0)


def em_kernel(total_subjects, total_supports, ny, nz,
              obs_hbm, noise_hbm, times_hbm, absorption_hbm, elimination_hbm, volume_hbm, weights_hbm, counts_hbm,
              new_ref, loglik_ref,
              obs_v, noise_v, times_v, absorption_v, elimination_v, volume_v, weights_v, counts_v, load_sem,
              curves, current, linear_v, square_v, features_v, log_lik_even, log_lik_odd, tile, log_scale,
              mix_own, mix_start, mix_pair, mix_near, mix_far, factor,
              sums, y_in, z_out, z_in, held,
              mix_send, mix_recv, y_send, y_recv, z_send, z_recv, gz_send, gz_recv, gy_send, gy_recv):
    samples = obs_v.shape[0]
    all_reps, subjects = counts_v.shape
    reps = all_reps
    half = subjects // 2
    per_half = half // BLOCK
    supports = weights_v.shape[1]
    width = supports // CHUNKS
    piece_rows, piece = reps // nz, width // ny
    subj, supp = lax.axis_index("subj"), lax.axis_index("supp")
    y, z = lax.rem(subj, ny), lax.div(subj, ny)
    core = lax.rem(supp, 2)
    core_peer = {"subj": subj, "supp": supp + 1 - 2 * core}
    x_peer = {"subj": subj, "supp": lax.rem(supp + 2, 4)}
    y_peer = {"subj": subj + 1 - 2 * y, "supp": supp}
    z_at = [lax.rem(z + d, nz) for d in range(nz)]
    z_peers = [{"subj": z_at[d] * ny + y, "supp": supp} for d in range(nz)]
    in_flight = {}
    mix_rows = lambda it: all_reps + PEAK_ROWS if it == 0 else all_reps

    loads = [pltpu.make_async_copy(src, dst, load_sem.at[k]) for k, (src, dst) in enumerate((
        (absorption_hbm, absorption_v), (elimination_hbm, elimination_v), (volume_hbm, volume_v),
        (weights_hbm, weights_v), (obs_hbm, obs_v), (noise_hbm, noise_v), (times_hbm, times_v),
        (counts_hbm, counts_v)))]
    for load in loads:
        load.start()

    def send(src, dst, send_sem, recv_sem, peer, key):
        if key in in_flight:
            in_flight.pop(key)()
        copy = pltpu.make_async_remote_copy(
            src_ref=src, dst_ref=dst, send_sem=send_sem, recv_sem=recv_sem,
            device_id=peer, device_id_type=pl.DeviceIdType.MESH)
        copy.start()
        in_flight[key] = copy.wait_send
        return copy

    def send_along_z(src_of, dst_of, send_sem, recv_sem, several, key):
        all_sent = pltpu.make_async_copy(several, several, send_sem)
        if key in in_flight:
            in_flight.pop(key)()
        for d in range(1, nz):
            pltpu.make_async_remote_copy(
                src_ref=src_of(d), dst_ref=dst_of(d), send_sem=send_sem, recv_sem=recv_sem,
                device_id=z_peers[d], device_id_type=pl.DeviceIdType.MESH).start()
        in_flight[key] = all_sent.wait
        return pltpu.make_async_copy(several, several, recv_sem)

    barrier = pltpu.get_barrier_semaphore()
    peers = [core_peer, x_peer, y_peer] + z_peers[1:]
    for peer in peers:
        pl.semaphore_signal(barrier, inc=1, device_id=peer, device_id_type=pl.DeviceIdType.MESH)

    for load in loads[:3]:
        load.wait()

    @pl.loop(0, supports // 512)
    def _(step):
        build_curves(absorption_v, elimination_v, volume_v, curves, step)

    for load in loads[3:]:
        load.wait()
    hi, lo = split(weights_v[...])
    current[...] = jnp.concatenate([hi, lo], axis=0)
    blocks = subjects // BLOCK
    starts = [pl.multiple_of((1 - core) * half + b * BLOCK, BLOCK) for b in range(per_half)]
    starts += [pl.multiple_of(core * half + b * BLOCK, BLOCK) for b in range(per_half)]
    columns = [pl.ds(at, BLOCK) for at in starts]
    offsets = {}

    def prepare(b):
        obs, noise = obs_v[:, columns[b]], noise_v[:, columns[b]]
        precision = 1.0 / (noise * noise)
        linear = obs * precision
        linear_v[...] = linear
        square_v[...] = -0.5 * precision
        offsets[b] = -0.5 * jnp.sum(obs * linear, axis=0, keepdims=True)
        scale = jnp.sum(jnp.log(noise), axis=0, keepdims=True)
        log_scale[:, columns[b]] = jnp.broadcast_to(scale, (PEAK_ROWS, BLOCK))

    def feature_rows(b, step):
        features = features_v.at[b % 2]
        for k in range(NT // FILL_STEPS // GROUP):
            first_row = pl.multiple_of(step * (NT // FILL_STEPS) + k * GROUP, GROUP)
            index = lax.broadcasted_iota(jnp.int32, (GROUP, BLOCK), 0) + first_row
            linear_part = jnp.zeros((GROUP, BLOCK), F32)
            square_part = jnp.zeros((GROUP, BLOCK), F32)
            for j in range(samples):
                hit = times_v[j:j + 1, columns[b]] == index
                linear_part = linear_part + jnp.where(hit, linear_v[j:j + 1, :], 0.0)
                square_part = square_part + jnp.where(hit, square_v[j:j + 1, :], 0.0)
            for base, part in ((0, linear_part), (NT, square_part)):
                hi, lo = split(part)
                for slot, value in ((0, hi), (1, lo), (2, hi)):
                    at = pl.ds(pl.multiple_of(slot * 2 * NT + base + first_row, GROUP), GROUP)
                    features[at, :] = value

    fill_step = supports // FILL_STEPS
    logs = (log_lik_even, log_lik_odd)

    prepare(0)

    @pl.loop(0, FILL_STEPS)
    def _(step):
        feature_rows(0, step)

    def fill_stage(b, peak_before):
        if b + 1 < blocks:
            prepare(b + 1)

        def one(step, carry):
            peak, mix = carry
            at = pl.ds(pl.multiple_of(step * fill_step, fill_step), fill_step)
            if b < blocks:
                part = jnp.dot(curves[at, :], features_v[b % 2], preferred_element_type=F32)
                logs[b % 2][at, :] = part
                peak = jnp.maximum(peak, jnp.max(part.reshape(fill_step // 8, 8, BLOCK), axis=0))
            if b > 0:
                like = jnp.exp(logs[(b - 1) % 2][at, :] - peak_before).astype(BF16)
                tile[at, columns[b - 1]] = like
                mix = mix + jnp.dot(current[:, at], like, preferred_element_type=F32)
            if b + 1 < blocks:
                feature_rows(b + 1, step)
            return peak, mix

        peak, mix = lax.fori_loop(0, FILL_STEPS, one, (
            jnp.full((8, BLOCK), -jnp.inf, F32), jnp.zeros((2 * all_reps, BLOCK), F32)))
        if b > 0:
            side = 1 - core if b - 1 < per_half else core
            within = slice((b - 1) % per_half * BLOCK, ((b - 1) % per_half + 1) * BLOCK)
            mix = mix[:all_reps] + mix[all_reps:]
            mix_start[0, side, :all_reps, within] = mix
            mix_start[0, side, all_reps:, within] = jnp.broadcast_to(
                peak_before + offsets[b - 1], (PEAK_ROWS, BLOCK))
        return jnp.max(peak, axis=0, keepdims=True)

    first = {}

    def start_exchange(it):
        to_send = pl.ds(0, mix_rows(it))
        first[it] = send(mix_start.at[it, 1 - core, to_send], mix_near.at[it, to_send], mix_send.at[0],
                         mix_recv.at[0], core_peer, ("mix", 0))

    peak = None
    for b in range(blocks + 1):
        peak = fill_stage(b, peak)
        if b == per_half:
            pl.semaphore_wait(barrier, len(peers))
            start_exchange(0)

    def stages_of(it):
        mixed = pl.ds(0, mix_rows(it))
        join = (lambda a, b: merge(a, b, reps)) if it == 0 else (lambda a, b: a + b)
        live = {}
        y_copies, z_copies, gz_copies, gy_copies = {}, {}, {}, {}

        def to_x():
            first[it].wait_recv()
            mix_pair[it, mixed] = join(mix_start[it, core, mixed], mix_near[it, mixed])
            live["x"] = send(mix_pair.at[it, mixed], mix_far.at[it, mixed], mix_send.at[2 + it],
                             mix_recv.at[2 + it], x_peer, ("mix", 2 + it))

        def to_core():
            live["x"].wait_recv()
            mix_own[it, core, mixed] = join(mix_pair[it, mixed], mix_far[it, mixed])
            live["core"] = send(mix_own.at[it, core, mixed], mix_own.at[it, core, mixed], mix_send.at[1],
                                mix_recv.at[1], core_peer, ("mix", 1))

        def respond():
            live["core"].wait_recv()
            parts = []
            for side in range(2):
                columns = slice(side * half, (side + 1) * half)
                mixture = mix_own[it, side, :reps, :]
                if it == 0:
                    peak = mix_own[0, side, reps:, :]
                    factor[:, columns] = jnp.exp(mix_start[0, side, reps:, :] - peak)
                    loglik_ref[:, columns] = (
                        peak[:1] + jnp.log(mixture / total_supports) - log_scale[:1, columns]
                    ) / samples - 0.5 * math.log(2.0 * math.pi)
                counts = counts_v[:, columns]
                drawn = counts > 0
                resp = jnp.where(drawn, counts.astype(F32) / jnp.where(drawn, mixture, 1.0), 0.0)
                parts.append(resp * factor[:1, columns])
            hi, lo = split(jnp.concatenate(parts, axis=1))
            live["resp"] = jnp.concatenate([hi, lo], axis=0)

        def compute(c):
            both = lax.dot_general(live["resp"], tile[c * width:(c + 1) * width, :],
                                   (((1,), (1,)), ((), ())), preferred_element_type=F32)
            part = both[:reps] + both[reps:]
            for a in range(ny):
                for b in range(nz):
                    sums[it, c, a, b] = part[b * piece_rows:(b + 1) * piece_rows, a * piece:(a + 1) * piece]
            y_copies[c] = send(sums.at[it, c, 1 - y], y_in.at[it, c], y_send.at[c],
                               y_recv.at[c], y_peer, ("y", c))

        def over_z(c):
            y_copies[c].wait_recv()
            z_out[it, c] = sums[it, c, y] + y_in[it, c]
            z_copies[c] = send_along_z(lambda d: z_out.at[it, c, z_at[d]], lambda d: z_in.at[it, c, d - 1],
                                       z_send.at[c], z_recv.at[c], z_in.at[it, c], ("z", c))

        def update(c):
            total = z_out[it, c, z]
            z_copies[c].wait()
            for d in range(1, nz):
                total = total + z_in[it, c, d - 1]
            if it == 0:
                rows = pl.ds(pl.multiple_of(z * piece_rows, piece_rows), piece_rows)
                before = weights_v[rows, pl.ds(pl.multiple_of(c * width + y * piece, piece), piece)]
            else:
                before = held[it - 1, c, y, z]
            held[it, c, y, z] = before * total / total_subjects
            gz_copies[c] = send_along_z(lambda d: held.at[it, c, y, z], lambda d: held.at[it, c, y, z],
                                        gz_send.at[c], gz_recv.at[c], z_in.at[it, c], ("gz", c))

        def over_y(c):
            gz_copies[c].wait()
            gy_copies[c] = send(held.at[it, c, y], held.at[it, c, y], gy_send.at[c],
                                gy_recv.at[c], y_peer, ("gy", c))

        def finish(c):
            gy_copies[c].wait_recv()
            now = jnp.concatenate([held[it, c, a].reshape(reps, piece) for a in range(ny)], axis=1)
            if it == ITERS - 1:
                new_ref[:, c * width:(c + 1) * width] = now
                return
            hi, lo = split(now)
            part = jnp.dot(jnp.concatenate([hi, lo], axis=0), tile[c * width:(c + 1) * width, :],
                           preferred_element_type=F32)
            live["mix"] = part if c == 0 else live["mix"] + part
            if c == CHUNKS - 1:
                mix = (live["mix"][:reps] + live["mix"][reps:]) * factor[:1, :]
                for side in range(2):
                    mix_start[it + 1, side, :reps, :] = mix[:, side * half:(side + 1) * half]
                start_exchange(it + 1)

        order = [(PACE * c, c, functools.partial(compute, c)) for c in range(CHUNKS)]
        order += [(c + late, c, functools.partial(stage, c)) for c in range(CHUNKS)
                  for late, stage in zip(LATE, (over_z, update, over_y, finish))]
        return [to_x, to_core, respond] + [stage for _, _, stage in sorted(order, key=lambda entry: entry[:2])]

    for it in range(ITERS):
        for stage in stages_of(it):
            stage()
    for wait in in_flight.values():
        wait()


def run_em(obs, noise, times, absorption, elimination, volume, weights, counts, ny, nz, sizes):
    reps, supports = weights.shape
    samples, subjects = obs.shape
    half = subjects // 2
    piece = (reps // nz, supports // (CHUNKS * ny))
    rows = reps + PEAK_ROWS
    dma = lambda *shape: pltpu.SemaphoreType.DMA(shape)
    vmem = lambda *shape: pltpu.VMEM(shape, F32)
    parts = (ITERS, CHUNKS)
    inputs = (obs, noise, times, absorption, elimination, volume, weights, counts)
    return pl.pallas_call(
        functools.partial(em_kernel, float(sizes[0]), float(sizes[1]), ny, nz),
        out_shape=[pltpu.VMEM((reps, supports), F32), pltpu.VMEM((reps, subjects), F32)],
        in_specs=[pl.BlockSpec(memory_space=pltpu.HBM)] * len(inputs),
        out_specs=[pl.BlockSpec(memory_space=pltpu.VMEM)] * 2,
        scratch_shapes=[pltpu.VMEM(a.shape, a.dtype) for a in inputs] + [
            dma(len(inputs)),
            pltpu.VMEM((supports, 6 * NT), BF16), pltpu.VMEM((2 * reps, supports), BF16),
            vmem(samples, BLOCK), vmem(samples, BLOCK), pltpu.VMEM((2, 6 * NT, BLOCK), BF16),
            vmem(supports, BLOCK), vmem(supports, BLOCK), pltpu.VMEM((supports, subjects), BF16),
            vmem(PEAK_ROWS, subjects),
            vmem(ITERS, 2, rows, half), vmem(ITERS, 2, rows, half), vmem(ITERS, rows, half),
            vmem(ITERS, rows, half), vmem(ITERS, rows, half), vmem(PEAK_ROWS, subjects),
            vmem(*parts, ny, nz, *piece), vmem(*parts, nz, *piece),
            vmem(*parts, nz, *piece), vmem(*parts, nz - 1, *piece),
            vmem(*parts, ny, nz, *piece),
            dma(2 + ITERS), dma(2 + ITERS), *[dma(CHUNKS)] * 8,
        ],
        compiler_params=pltpu.CompilerParams(collective_id=0, has_side_effects=True, vmem_limit_bytes=56 * MIB),
        name="em_steps",
    )(*inputs)


def hand_over(new, loglik):
    rows = 8

    def kernel(new_in, loglik_in, new_out, loglik_out, sem):
        copies = [pltpu.make_async_copy(new_in.at[pl.ds(k * rows, rows)], new_out.at[pl.ds(k * rows, rows)], sem.at[k])
                  for k in range(new_in.shape[0] // rows)]
        copies.append(pltpu.make_async_copy(loglik_in, loglik_out, sem.at[len(copies)]))
        for copy in copies:
            copy.start()
        for copy in copies:
            copy.wait()

    return pl.pallas_call(
        kernel,
        out_shape=[jax.ShapeDtypeStruct(new.shape, F32), jax.ShapeDtypeStruct(loglik.shape, F32)],
        in_specs=[pl.BlockSpec(memory_space=pltpu.VMEM)] * 2,
        out_specs=[pl.BlockSpec(memory_space=pltpu.HBM)] * 2,
        scratch_shapes=[pltpu.SemaphoreType.DMA((1 + new.shape[0] // rows,))],
        name="hand_over",
    )(new, loglik)


def plain_em(tile, mix, log_scale, counts, weights, samples, total_subjects, total_supports):
    reps = weights.shape[0]
    both = jnp.concatenate([mix[0], mix[1]], axis=1)
    local_peak = both[reps]
    peak = lax.pmax(local_peak, "supp")
    factor = jnp.exp(local_peak - peak)
    partial_mix = both[:reps]
    drawn = counts > 0
    current = weights
    loglik = None
    for it in range(ITERS):
        if it > 0:
            hi, lo = split(current)
            pair = jnp.dot(jnp.concatenate([hi, lo], axis=0), tile, preferred_element_type=F32)
            partial_mix = pair[:reps] + pair[reps:]
        mixture = lax.psum(partial_mix * factor, "supp")
        if it == 0:
            loglik = (peak + jnp.log(mixture / total_supports) - log_scale[:1]) / samples
            loglik = loglik - 0.5 * math.log(2.0 * math.pi)
        resp = jnp.where(drawn, counts.astype(F32) / jnp.where(drawn, mixture, 1.0), 0.0) * factor
        hi, lo = split(resp)
        pair = lax.dot_general(jnp.concatenate([hi, lo], axis=0), tile, (((1,), (1,)), ((), ())),
                               preferred_element_type=F32)
        current = current * lax.psum(pair[:reps] + pair[reps:], "subj") / total_subjects
    return current, loglik


def body(observations, noise_scale, sample_times, counts, absorption, elimination, volume, weights):
    n_subj, n_supp = lax.axis_size("subj"), lax.axis_size("supp")
    subjects, samples = observations.shape
    sizes = (subjects * n_subj, weights.shape[1] * n_supp)
    inputs = (observations.T, noise_scale.T, sample_times.T,
              absorption[None, :], elimination[None, :], volume[None, :], weights)
    if (n_subj, n_supp) == (8, 4):
        new, loglik = run_em(*inputs, counts, 2, 4, sizes)
        return hand_over(pltpu.with_memory_space_constraint(new, pltpu.VMEM), pltpu.with_memory_space_constraint(loglik, pltpu.VMEM))
    return plain_em(*make_tile(*inputs), counts, weights, samples, *sizes)


def solution(mesh):
    return jax.shard_map(
        body,
        mesh=mesh,
        in_specs=(
            P("subj", None),
            P("subj", None),
            P("subj", None),
            P(None, "subj"),
            P("supp"),
            P("supp"),
            P("supp"),
            P(None, "supp"),
        ),
        out_specs=(P(None, "supp"), P(None, "subj")),
        check_vma=False,
    )
```

```python
import functools
import math

import jax
import jax.numpy as jnp
from jax import lax
from jax.experimental import pallas as pl
from jax.experimental.pallas import tpu as pltpu
from jax.sharding import PartitionSpec as P

NT = 128
HORIZON = 24.0
ITERS = 2
BLOCK = 256
KSTEP = 2048
CHUNKS = 8
FILL_STEPS = 2
GROUP = 32
PEAK_ROWS = 8
LATE = (3.2, 10.7, 18.2, 25.7)
PACE = 0.62
MIB = 1 << 20
F32 = jnp.float32
BF16 = jnp.bfloat16


def split(x):
    hi = x.astype(BF16)
    return hi, (x - hi.astype(F32)).astype(BF16)


def build_curves(absorption_ref, elimination_ref, volume_ref, curves, step):
    step_size = 512
    grid_rows = lax.broadcasted_iota(jnp.int32, (NT, step_size), 0).astype(F32)
    time_grid = (grid_rows + 1.0) * (HORIZON / NT)

    at = pl.ds(pl.multiple_of(step * step_size, step_size), step_size)
    rate_in = absorption_ref[:, at]
    rate_out = elimination_ref[:, at]
    amplitude = rate_in / (volume_ref[:, at] * (rate_in - rate_out))
    rows = amplitude * (jnp.exp(-rate_out * time_grid) - jnp.exp(-rate_in * time_grid))
    columns = rows.T
    for half, part in ((0, columns), (NT, columns * columns)):
        hi, lo = split(part)
        curves[at, half:half + NT] = hi
        curves[at, 2 * NT + half:3 * NT + half] = hi
        curves[at, 4 * NT + half:5 * NT + half] = lo


def block_mixture(obs, noise, times, curves, current, log_lik, tile_ref, columns):
    supports = log_lik.shape[0]
    steps = supports // KSTEP
    precision = 1.0 / (noise * noise)
    linear = obs * precision
    square = -0.5 * precision
    grid_index = lax.broadcasted_iota(jnp.int32, (NT, BLOCK), 0)
    linear_part = jnp.zeros((NT, BLOCK), F32)
    square_part = jnp.zeros((NT, BLOCK), F32)
    for j in range(obs.shape[0]):
        hit = times[j:j + 1, :] == grid_index
        linear_part = linear_part + jnp.where(hit, linear[j:j + 1, :], 0.0)
        square_part = square_part + jnp.where(hit, square[j:j + 1, :], 0.0)
    offset = -0.5 * jnp.sum(obs * obs * precision, axis=0, keepdims=True)
    log_scale = jnp.sum(jnp.log(noise), axis=0, keepdims=True)
    hi, lo = split(jnp.concatenate([linear_part, square_part], axis=0))
    features = jnp.concatenate([hi, lo, hi], axis=0)

    def one_log(step, peak):
        at = pl.ds(pl.multiple_of(step * KSTEP, KSTEP), KSTEP)
        part = jnp.dot(curves[at, :], features, preferred_element_type=F32)
        log_lik[at, :] = part
        return jnp.maximum(peak, jnp.max(part.reshape(KSTEP // 8, 8, BLOCK), axis=0))

    peak = lax.fori_loop(0, steps, one_log, jnp.full((8, BLOCK), -jnp.inf, F32))
    peak = jnp.max(peak, axis=0, keepdims=True)

    def one_tile(step, mix):
        at = pl.ds(pl.multiple_of(step * KSTEP, KSTEP), KSTEP)
        like = jnp.exp(log_lik[at, :] - peak).astype(BF16)
        tile_ref[at, columns] = like
        return mix + jnp.dot(current[:, at], like, preferred_element_type=F32)

    mix = lax.fori_loop(0, steps, one_tile, jnp.zeros((current.shape[0], BLOCK), F32))
    return mix, peak + offset, log_scale


def tile_kernel(obs_ref, noise_ref, times_ref, absorption_ref, elimination_ref, volume_ref,
                weights_ref, tile_ref, mix_ref, scale_ref, curves, current, log_lik):
    reps = weights_ref.shape[0]

    @pl.when(pl.program_id(0) == 0)
    def _():
        hi, lo = split(weights_ref[...])
        current[...] = jnp.concatenate([hi, lo], axis=0)
        @pl.loop(0, absorption_ref.shape[1] // 512)
        def _(step):
            build_curves(absorption_ref, elimination_ref, volume_ref, curves, step)

    mix, peak, log_scale = block_mixture(obs_ref[...], noise_ref[...], times_ref[...], curves, current,
                                         log_lik, tile_ref, slice(None))
    mix_ref[0, :reps, :] = mix[:reps] + mix[reps:]
    mix_ref[0, reps:, :] = jnp.broadcast_to(peak, (PEAK_ROWS, BLOCK))
    scale_ref[...] = jnp.broadcast_to(log_scale, (PEAK_ROWS, BLOCK))


def make_tile(obs, noise, times, absorption, elimination, volume, weights):
    samples, subjects = obs.shape
    reps, supports = weights.shape
    half = subjects // 2
    per_half = half // BLOCK
    by_subject = pl.BlockSpec((samples, BLOCK), lambda b: (0, b))
    whole = lambda shape: pl.BlockSpec(shape, lambda b: (0, 0))
    return pl.pallas_call(
        tile_kernel,
        grid=(subjects // BLOCK,),
        in_specs=[by_subject] * 3 + [whole((1, supports))] * 3 + [whole((reps, supports))],
        out_specs=[
            pl.BlockSpec((supports, BLOCK), lambda b: (0, b)),
            pl.BlockSpec((1, reps + PEAK_ROWS, BLOCK), lambda b: (b // per_half, 0, b % per_half)),
            pl.BlockSpec((PEAK_ROWS, BLOCK), lambda b: (0, b)),
        ],
        out_shape=[
            jax.ShapeDtypeStruct((supports, subjects), BF16),
            jax.ShapeDtypeStruct((2, reps + PEAK_ROWS, half), F32),
            jax.ShapeDtypeStruct((PEAK_ROWS, subjects), F32),
        ],
        scratch_shapes=[
            pltpu.VMEM((supports, 6 * NT), BF16),
            pltpu.VMEM((2 * reps, supports), BF16),
            pltpu.VMEM((supports, BLOCK), F32),
        ],
        compiler_params=pltpu.CompilerParams(vmem_limit_bytes=32 * MIB),
        name="make_tile",
    )(obs, noise, times, absorption, elimination, volume, weights)


def merge(mine, other, reps):
    peak_a, peak_b = mine[reps:], other[reps:]
    peak = jnp.maximum(peak_a, peak_b)
    scale_a, scale_b = jnp.exp(peak_a - peak)[:1], jnp.exp(peak_b - peak)[:1]
    return jnp.concatenate([mine[:reps] * scale_a + other[:reps] * scale_b, peak], axis=0)


def em_kernel(total_subjects, total_supports, ny, nz,
              obs_hbm, noise_hbm, times_hbm, absorption_hbm, elimination_hbm, volume_hbm, weights_hbm, counts_hbm,
              new_ref, loglik_ref,
              obs_v, noise_v, times_v, absorption_v, elimination_v, volume_v, weights_v, counts_v, load_sem,
              curves, current, linear_v, square_v, features_v, log_lik_even, log_lik_odd, tile, log_scale,
              mix_own, mix_start, mix_pair, mix_near, mix_far, factor,
              sums, y_in, z_out, z_in, held,
              mix_send, mix_recv, chunk_send, y_recv, z_recv, gz_recv, gy_recv):
    samples = obs_v.shape[0]
    all_reps, subjects = counts_v.shape
    reps = all_reps
    half = subjects // 2
    per_half = half // BLOCK
    supports = weights_v.shape[1]
    width = supports // CHUNKS
    piece_rows, piece = reps // nz, width // ny
    subj, supp = lax.axis_index("subj"), lax.axis_index("supp")
    y, z = lax.rem(subj, ny), lax.div(subj, ny)
    core = lax.rem(supp, 2)
    core_peer = {"subj": subj, "supp": supp + 1 - 2 * core}
    x_peer = {"subj": subj, "supp": lax.rem(supp + 2, 4)}
    y_peer = {"subj": subj + 1 - 2 * y, "supp": supp}
    z_at = [lax.rem(z + d, nz) for d in range(nz)]
    z_peers = [{"subj": z_at[d] * ny + y, "supp": supp} for d in range(nz)]
    in_flight = {}
    mix_rows = lambda it: all_reps + PEAK_ROWS if it == 0 else all_reps

    loads = [pltpu.make_async_copy(src, dst, load_sem.at[k]) for k, (src, dst) in enumerate((
        (absorption_hbm, absorption_v), (elimination_hbm, elimination_v), (volume_hbm, volume_v),
        (obs_hbm, obs_v), (noise_hbm, noise_v), (times_hbm, times_v), (weights_hbm, weights_v),
        (counts_hbm, counts_v)))]
    for load in loads:
        load.start()

    def send(src, dst, send_sem, recv_sem, peer, key):
        if key in in_flight:
            in_flight.pop(key)()
        copy = pltpu.make_async_remote_copy(
            src_ref=src, dst_ref=dst, send_sem=send_sem, recv_sem=recv_sem,
            device_id=peer, device_id_type=pl.DeviceIdType.MESH)
        copy.start()
        in_flight[key] = copy.wait_send
        return copy

    def send_chunk(src, dst, send_sem, recv_sem, peer, it, kind, every):
        if (it - 1, kind) in in_flight:
            in_flight.pop((it - 1, kind))()
        copy = pltpu.make_async_remote_copy(
            src_ref=src, dst_ref=dst, send_sem=send_sem, recv_sem=recv_sem,
            device_id=peer, device_id_type=pl.DeviceIdType.MESH)
        copy.start()
        in_flight[it, kind] = lambda: pltpu.make_async_copy(every, every, send_sem).wait()
        return copy

    def send_along_z(src_of, dst_of, send_sem, recv_sem, it, c, kind):
        for d in range(1, nz):
            send_chunk(src_of(d), dst_of(d), send_sem, recv_sem, z_peers[d], it, kind, z_in.at[it])
        return pltpu.make_async_copy(z_in.at[it, c], z_in.at[it, c], recv_sem)

    barrier = pltpu.get_barrier_semaphore()
    peers = [core_peer, x_peer, y_peer] + z_peers[1:]
    for peer in peers:
        pl.semaphore_signal(barrier, inc=1, device_id=peer, device_id_type=pl.DeviceIdType.MESH)

    for load in loads[:6]:
        load.wait()
    blocks = subjects // BLOCK
    starts = [pl.multiple_of((1 - core) * half + b * BLOCK, BLOCK) for b in range(per_half)]
    starts += [pl.multiple_of(core * half + b * BLOCK, BLOCK) for b in range(per_half)]
    columns = [pl.ds(at, BLOCK) for at in starts]
    offsets = {}

    def prepare(b):
        obs, noise = obs_v[:, columns[b]], noise_v[:, columns[b]]
        precision = 1.0 / (noise * noise)
        linear = obs * precision
        linear_v[...] = linear
        square_v[...] = -0.5 * precision
        offsets[b] = -0.5 * jnp.sum(obs * linear, axis=0, keepdims=True)
        scale = jnp.sum(jnp.log(noise), axis=0, keepdims=True)
        log_scale[:, columns[b]] = jnp.broadcast_to(scale, (PEAK_ROWS, BLOCK))

    def feature_rows(b, step):
        features = features_v.at[b % 2]
        for k in range(NT // FILL_STEPS // GROUP):
            first_row = pl.multiple_of(step * (NT // FILL_STEPS) + k * GROUP, GROUP)
            index = lax.broadcasted_iota(jnp.int32, (GROUP, BLOCK), 0) + first_row
            linear_part = jnp.zeros((GROUP, BLOCK), F32)
            square_part = jnp.zeros((GROUP, BLOCK), F32)
            for j in range(samples):
                hit = times_v[j:j + 1, columns[b]] == index
                linear_part = linear_part + jnp.where(hit, linear_v[j:j + 1, :], 0.0)
                square_part = square_part + jnp.where(hit, square_v[j:j + 1, :], 0.0)
            for base, part in ((0, linear_part), (NT, square_part)):
                hi, lo = split(part)
                for slot, value in ((0, hi), (1, lo), (2, hi)):
                    at = pl.ds(pl.multiple_of(slot * 2 * NT + base + first_row, GROUP), GROUP)
                    features[at, :] = value

    fill_step = supports // FILL_STEPS
    logs = (log_lik_even, log_lik_odd)

    prepare(0)

    curve_steps = supports // 512 // FILL_STEPS

    @pl.loop(0, FILL_STEPS)
    def _(step):
        for k in range(curve_steps):
            build_curves(absorption_v, elimination_v, volume_v, curves, step * curve_steps + k)
        feature_rows(0, step)

    for load in loads[6:]:
        load.wait()
    hi, lo = split(weights_v[...])
    current[...] = jnp.concatenate([hi, lo], axis=0)

    def fill_stage(b, peak_before):
        if b + 1 < blocks:
            prepare(b + 1)

        def one(step, carry):
            peak, mix = carry
            at = pl.ds(pl.multiple_of(step * fill_step, fill_step), fill_step)
            if b < blocks:
                part = jnp.dot(curves[at, :], features_v[b % 2], preferred_element_type=F32)
                logs[b % 2][at, :] = part
                peak = jnp.maximum(peak, jnp.max(part.reshape(fill_step // 8, 8, BLOCK), axis=0))
            if b > 0:
                like = jnp.exp(logs[(b - 1) % 2][at, :] - peak_before).astype(BF16)
                tile[at, columns[b - 1]] = like
                mix = mix + jnp.dot(current[:, at], like, preferred_element_type=F32)
            if b + 1 < blocks:
                feature_rows(b + 1, step)
            return peak, mix

        peak, mix = lax.fori_loop(0, FILL_STEPS, one, (
            jnp.full((8, BLOCK), -jnp.inf, F32), jnp.zeros((2 * all_reps, BLOCK), F32)))
        if b > 0:
            side = 1 - core if b - 1 < per_half else core
            within = slice((b - 1) % per_half * BLOCK, ((b - 1) % per_half + 1) * BLOCK)
            mix = mix[:all_reps] + mix[all_reps:]
            mix_start[0, side, :all_reps, within] = mix
            mix_start[0, side, all_reps:, within] = jnp.broadcast_to(
                peak_before + offsets[b - 1], (PEAK_ROWS, BLOCK))
        return jnp.max(peak, axis=0, keepdims=True)

    first = {}

    def start_exchange(it):
        to_send = pl.ds(0, mix_rows(it))
        first[it] = send(mix_start.at[it, 1 - core, to_send], mix_near.at[it, to_send], mix_send.at[0],
                         mix_recv.at[0], core_peer, ("mix", 0))

    def stages_of(it):
        mixed = pl.ds(0, mix_rows(it))
        join = (lambda a, b: merge(a, b, reps)) if it == 0 else (lambda a, b: a + b)
        live = {}
        x_copies, core_copies, y_copies, z_copies, gz_copies, gy_copies = {}, {}, {}, {}, {}, {}

        def to_x(p):
            within = pl.ds(p * BLOCK, BLOCK)
            if p == 0:
                first[it].wait_recv()
            pair = mix_pair.at[it, mixed, within]
            pair[...] = join(mix_start[it, core, mixed, within], mix_near[it, mixed, within])
            at = 1 + per_half * (1 + it) + p
            x_copies[p] = send(pair, mix_far.at[it, mixed, within], mix_send.at[at], mix_recv.at[at], x_peer, ("mix", at))

        def to_core(p):
            within = pl.ds(p * BLOCK, BLOCK)
            x_copies[p].wait_recv()
            own = mix_own.at[it, core, mixed, within]
            own[...] = join(mix_pair[it, mixed, within], mix_far[it, mixed, within])
            core_copies[p] = send(own, own, mix_send.at[1 + p], mix_recv.at[1 + p], core_peer, ("mix", 1 + p))

        def respond():
            for copy in core_copies.values():
                copy.wait_recv()
            parts = []
            for side in range(2):
                columns = slice(side * half, (side + 1) * half)
                mixture = mix_own[it, side, :reps, :]
                if it == 0:
                    peak = mix_own[0, side, reps:, :]
                    factor[:, columns] = jnp.exp(mix_start[0, side, reps:, :] - peak)
                    loglik_ref[:, columns] = (
                        peak[:1] + jnp.log(mixture / total_supports) - log_scale[:1, columns]
                    ) / samples - 0.5 * math.log(2.0 * math.pi)
                counts = counts_v[:, columns]
                drawn = counts > 0
                resp = jnp.where(drawn, counts.astype(F32) / jnp.where(drawn, mixture, 1.0), 0.0)
                parts.append(resp * factor[:1, columns])
            hi, lo = split(jnp.concatenate(parts, axis=1))
            live["resp"] = jnp.concatenate([hi, lo], axis=0)

        def compute(c):
            both = lax.dot_general(live["resp"], tile[c * width:(c + 1) * width, :],
                                   (((1,), (1,)), ((), ())), preferred_element_type=F32)
            part = both[:reps] + both[reps:]
            for a in range(ny):
                for b in range(nz):
                    sums[it, c, a, b] = part[b * piece_rows:(b + 1) * piece_rows, a * piece:(a + 1) * piece]
            y_copies[c] = send_chunk(sums.at[it, c, 1 - y], y_in.at[it, c], chunk_send.at[0],
                                     y_recv.at[c], y_peer, it, "y", y_in.at[it])

        def over_z(c):
            y_copies[c].wait_recv()
            z_out[it, c] = sums[it, c, y] + y_in[it, c]
            z_copies[c] = send_along_z(lambda d: z_out.at[it, c, z_at[d]], lambda d: z_in.at[it, c, d - 1],
                                       chunk_send.at[1], z_recv.at[c], it, c, "z")

        def update(c):
            total = z_out[it, c, z]
            z_copies[c].wait()
            for d in range(1, nz):
                total = total + z_in[it, c, d - 1]
            if it == 0:
                rows = pl.ds(pl.multiple_of(z * piece_rows, piece_rows), piece_rows)
                before = weights_v[rows, pl.ds(pl.multiple_of(c * width + y * piece, piece), piece)]
            else:
                before = held[it - 1, c, y, z]
            held[it, c, y, z] = before * total / total_subjects
            gz_copies[c] = send_along_z(lambda d: held.at[it, c, y, z], lambda d: held.at[it, c, y, z],
                                        chunk_send.at[2], gz_recv.at[c], it, c, "gz")

        def over_y(c):
            gz_copies[c].wait()
            gy_copies[c] = send_chunk(held.at[it, c, y], held.at[it, c, y], chunk_send.at[3],
                                      gy_recv.at[c], y_peer, it, "gy", y_in.at[it])

        def finish(c):
            gy_copies[c].wait_recv()
            now = jnp.concatenate([held[it, c, a].reshape(reps, piece) for a in range(ny)], axis=1)
            if it == ITERS - 1:
                new_ref[:, c * width:(c + 1) * width] = now
                return
            hi, lo = split(now)
            both = jnp.concatenate([hi, lo], axis=0)
            for side in (1 - core, core):
                at = pl.ds(pl.multiple_of(side * half, half), half)
                part = jnp.dot(both, tile[c * width:(c + 1) * width, at], preferred_element_type=F32)
                key = "mix_own" if side is core else "mix_other"
                live[key] = part if c == 0 else live[key] + part
                if c == CHUNKS - 1:
                    mix_start[it + 1, side, :reps, :] = (live[key][:reps] + live[key][reps:]) * factor[:1, at]
                    if side is not core:
                        start_exchange(it + 1)

        order = [(PACE * c, c, functools.partial(compute, c)) for c in range(CHUNKS)]
        order += [(c + late, c, functools.partial(stage, c)) for c in range(CHUNKS)
                  for late, stage in zip(LATE, (over_z, update, over_y, finish))]
        halves = range(per_half)
        return ([functools.partial(to_x, p) for p in halves], [functools.partial(to_core, p) for p in halves]
                + [respond] + [stage for _, _, stage in sorted(order, key=lambda entry: entry[:2])])

    peak = None
    for it in range(ITERS):
        sends, rest = stages_of(it)
        if it == 0:
            for b in range(blocks + 1):
                peak = fill_stage(b, peak)
                if b == per_half:
                    pl.semaphore_wait(barrier, len(peers))
                    start_exchange(0)
                if b > per_half:
                    sends[b - 1 - per_half]()
            sends = []
        for stage in sends + rest:
            stage()
    for wait in in_flight.values():
        wait()


def run_em(obs, noise, times, absorption, elimination, volume, weights, counts, ny, nz, sizes):
    reps, supports = weights.shape
    samples, subjects = obs.shape
    half = subjects // 2
    piece = (reps // nz, supports // (CHUNKS * ny))
    rows = reps + PEAK_ROWS
    dma = lambda *shape: pltpu.SemaphoreType.DMA(shape)
    vmem = lambda *shape: pltpu.VMEM(shape, F32)
    parts = (ITERS, CHUNKS)
    inputs = (obs, noise, times, absorption, elimination, volume, weights, counts)
    return pl.pallas_call(
        functools.partial(em_kernel, float(sizes[0]), float(sizes[1]), ny, nz),
        out_shape=[pltpu.VMEM((reps, supports), F32), pltpu.VMEM((reps, subjects), F32)],
        in_specs=[pl.BlockSpec(memory_space=pltpu.HBM)] * len(inputs),
        out_specs=[pl.BlockSpec(memory_space=pltpu.VMEM)] * 2,
        scratch_shapes=[pltpu.VMEM(a.shape, a.dtype) for a in inputs] + [
            dma(len(inputs)),
            pltpu.VMEM((supports, 6 * NT), BF16), pltpu.VMEM((2 * reps, supports), BF16),
            vmem(samples, BLOCK), vmem(samples, BLOCK), pltpu.VMEM((2, 6 * NT, BLOCK), BF16),
            vmem(supports, BLOCK), vmem(supports, BLOCK), pltpu.VMEM((supports, subjects), BF16),
            vmem(PEAK_ROWS, subjects),
            vmem(ITERS, 2, rows, half), vmem(ITERS, 2, rows, half), vmem(ITERS, rows, half),
            vmem(ITERS, rows, half), vmem(ITERS, rows, half), vmem(PEAK_ROWS, subjects),
            vmem(*parts, ny, nz, *piece), vmem(*parts, nz, *piece),
            vmem(*parts, nz, *piece), vmem(*parts, nz - 1, *piece),
            vmem(*parts, ny, nz, *piece),
            *[dma(1 + (1 + ITERS) * (half // BLOCK))] * 2, dma(4), *[dma(CHUNKS)] * 4,
        ],
        compiler_params=pltpu.CompilerParams(collective_id=0, has_side_effects=True, vmem_limit_bytes=56 * MIB),
        name="em_steps",
    )(*inputs)


def hand_over(new, loglik):
    rows = 8

    def kernel(new_in, loglik_in, new_out, loglik_out, sem):
        copies = [pltpu.make_async_copy(new_in.at[pl.ds(k * rows, rows)], new_out.at[pl.ds(k * rows, rows)], sem.at[k])
                  for k in range(new_in.shape[0] // rows)]
        copies.append(pltpu.make_async_copy(loglik_in, loglik_out, sem.at[len(copies)]))
        for copy in copies:
            copy.start()
        for copy in copies:
            copy.wait()

    return pl.pallas_call(
        kernel,
        out_shape=[jax.ShapeDtypeStruct(new.shape, F32), jax.ShapeDtypeStruct(loglik.shape, F32)],
        in_specs=[pl.BlockSpec(memory_space=pltpu.VMEM)] * 2,
        out_specs=[pl.BlockSpec(memory_space=pltpu.HBM)] * 2,
        scratch_shapes=[pltpu.SemaphoreType.DMA((1 + new.shape[0] // rows,))],
        name="hand_over",
    )(new, loglik)


def plain_em(tile, mix, log_scale, counts, weights, samples, total_subjects, total_supports):
    reps = weights.shape[0]
    both = jnp.concatenate([mix[0], mix[1]], axis=1)
    local_peak = both[reps]
    peak = lax.pmax(local_peak, "supp")
    factor = jnp.exp(local_peak - peak)
    partial_mix = both[:reps]
    drawn = counts > 0
    current = weights
    loglik = None
    for it in range(ITERS):
        if it > 0:
            hi, lo = split(current)
            pair = jnp.dot(jnp.concatenate([hi, lo], axis=0), tile, preferred_element_type=F32)
            partial_mix = pair[:reps] + pair[reps:]
        mixture = lax.psum(partial_mix * factor, "supp")
        if it == 0:
            loglik = (peak + jnp.log(mixture / total_supports) - log_scale[:1]) / samples
            loglik = loglik - 0.5 * math.log(2.0 * math.pi)
        resp = jnp.where(drawn, counts.astype(F32) / jnp.where(drawn, mixture, 1.0), 0.0) * factor
        hi, lo = split(resp)
        pair = lax.dot_general(jnp.concatenate([hi, lo], axis=0), tile, (((1,), (1,)), ((), ())),
                               preferred_element_type=F32)
        current = current * lax.psum(pair[:reps] + pair[reps:], "subj") / total_subjects
    return current, loglik


def body(observations, noise_scale, sample_times, counts, absorption, elimination, volume, weights):
    n_subj, n_supp = lax.axis_size("subj"), lax.axis_size("supp")
    subjects, samples = observations.shape
    sizes = (subjects * n_subj, weights.shape[1] * n_supp)
    inputs = (observations.T, noise_scale.T, sample_times.T,
              absorption[None, :], elimination[None, :], volume[None, :], weights)
    if (n_subj, n_supp) == (8, 4):
        new, loglik = run_em(*inputs, counts, 2, 4, sizes)
        return hand_over(pltpu.with_memory_space_constraint(new, pltpu.VMEM), pltpu.with_memory_space_constraint(loglik, pltpu.VMEM))
    return plain_em(*make_tile(*inputs), counts, weights, samples, *sizes)


def solution(mesh):
    return jax.shard_map(
        body,
        mesh=mesh,
        in_specs=(
            P("subj", None),
            P("subj", None),
            P("subj", None),
            P(None, "subj"),
            P("supp"),
            P("supp"),
            P("supp"),
            P(None, "supp"),
        ),
        out_specs=(P(None, "supp"), P(None, "subj")),
        check_vma=False,
    )
```

```python
import functools
import math

import jax
import jax.numpy as jnp
from jax import lax
from jax.experimental import pallas as pl
from jax.experimental.pallas import tpu as pltpu
from jax.sharding import PartitionSpec as P

NT = 128
HORIZON = 24.0
ITERS = 2
BLOCK = 256
KSTEP = 2048
CHUNKS = 8
FILL_STEPS = 2
GROUP = 32
PEAK_ROWS = 8
LATE = (3.2, 10.7, 18.2, 25.7)
PACE = 0.62
MIB = 1 << 20
F32 = jnp.float32
BF16 = jnp.bfloat16


def split(x):
    hi = x.astype(BF16)
    return hi, (x - hi.astype(F32)).astype(BF16)


def build_curves(absorption_ref, elimination_ref, volume_ref, curves, step):
    step_size = 512
    grid_rows = lax.broadcasted_iota(jnp.int32, (NT, step_size), 0).astype(F32)
    time_grid = (grid_rows + 1.0) * (HORIZON / NT)

    at = pl.ds(pl.multiple_of(step * step_size, step_size), step_size)
    rate_in = absorption_ref[:, at]
    rate_out = elimination_ref[:, at]
    amplitude = rate_in / (volume_ref[:, at] * (rate_in - rate_out))
    rows = amplitude * (jnp.exp(-rate_out * time_grid) - jnp.exp(-rate_in * time_grid))
    columns = rows.T
    for half, part in ((0, columns), (NT, columns * columns)):
        hi, lo = split(part)
        curves[at, half:half + NT] = hi
        curves[at, 2 * NT + half:3 * NT + half] = hi
        curves[at, 4 * NT + half:5 * NT + half] = lo


def block_mixture(obs, noise, times, curves, current, log_lik, tile_ref, columns):
    supports = log_lik.shape[0]
    steps = supports // KSTEP
    precision = 1.0 / (noise * noise)
    linear = obs * precision
    square = -0.5 * precision
    grid_index = lax.broadcasted_iota(jnp.int32, (NT, BLOCK), 0)
    linear_part = jnp.zeros((NT, BLOCK), F32)
    square_part = jnp.zeros((NT, BLOCK), F32)
    for j in range(obs.shape[0]):
        hit = times[j:j + 1, :] == grid_index
        linear_part = linear_part + jnp.where(hit, linear[j:j + 1, :], 0.0)
        square_part = square_part + jnp.where(hit, square[j:j + 1, :], 0.0)
    offset = -0.5 * jnp.sum(obs * obs * precision, axis=0, keepdims=True)
    log_scale = jnp.sum(jnp.log(noise), axis=0, keepdims=True)
    hi, lo = split(jnp.concatenate([linear_part, square_part], axis=0))
    features = jnp.concatenate([hi, lo, hi], axis=0)

    def one_log(step, peak):
        at = pl.ds(pl.multiple_of(step * KSTEP, KSTEP), KSTEP)
        part = jnp.dot(curves[at, :], features, preferred_element_type=F32)
        log_lik[at, :] = part
        return jnp.maximum(peak, jnp.max(part.reshape(KSTEP // 8, 8, BLOCK), axis=0))

    peak = lax.fori_loop(0, steps, one_log, jnp.full((8, BLOCK), -jnp.inf, F32))
    peak = jnp.max(peak, axis=0, keepdims=True)

    def one_tile(step, mix):
        at = pl.ds(pl.multiple_of(step * KSTEP, KSTEP), KSTEP)
        like = jnp.exp(log_lik[at, :] - peak).astype(BF16)
        tile_ref[at, columns] = like
        return mix + jnp.dot(current[:, at], like, preferred_element_type=F32)

    mix = lax.fori_loop(0, steps, one_tile, jnp.zeros((current.shape[0], BLOCK), F32))
    return mix, peak + offset, log_scale


def tile_kernel(obs_ref, noise_ref, times_ref, absorption_ref, elimination_ref, volume_ref,
                weights_ref, tile_ref, mix_ref, scale_ref, curves, current, log_lik):
    reps = weights_ref.shape[0]

    @pl.when(pl.program_id(0) == 0)
    def _():
        hi, lo = split(weights_ref[...])
        current[...] = jnp.concatenate([hi, lo], axis=0)
        @pl.loop(0, absorption_ref.shape[1] // 512)
        def _(step):
            build_curves(absorption_ref, elimination_ref, volume_ref, curves, step)

    mix, peak, log_scale = block_mixture(obs_ref[...], noise_ref[...], times_ref[...], curves, current,
                                         log_lik, tile_ref, slice(None))
    mix_ref[0, :reps, :] = mix[:reps] + mix[reps:]
    mix_ref[0, reps:, :] = jnp.broadcast_to(peak, (PEAK_ROWS, BLOCK))
    scale_ref[...] = jnp.broadcast_to(log_scale, (PEAK_ROWS, BLOCK))


def make_tile(obs, noise, times, absorption, elimination, volume, weights):
    samples, subjects = obs.shape
    reps, supports = weights.shape
    half = subjects // 2
    per_half = half // BLOCK
    by_subject = pl.BlockSpec((samples, BLOCK), lambda b: (0, b))
    whole = lambda shape: pl.BlockSpec(shape, lambda b: (0, 0))
    return pl.pallas_call(
        tile_kernel,
        grid=(subjects // BLOCK,),
        in_specs=[by_subject] * 3 + [whole((1, supports))] * 3 + [whole((reps, supports))],
        out_specs=[
            pl.BlockSpec((supports, BLOCK), lambda b: (0, b)),
            pl.BlockSpec((1, reps + PEAK_ROWS, BLOCK), lambda b: (b // per_half, 0, b % per_half)),
            pl.BlockSpec((PEAK_ROWS, BLOCK), lambda b: (0, b)),
        ],
        out_shape=[
            jax.ShapeDtypeStruct((supports, subjects), BF16),
            jax.ShapeDtypeStruct((2, reps + PEAK_ROWS, half), F32),
            jax.ShapeDtypeStruct((PEAK_ROWS, subjects), F32),
        ],
        scratch_shapes=[
            pltpu.VMEM((supports, 6 * NT), BF16),
            pltpu.VMEM((2 * reps, supports), BF16),
            pltpu.VMEM((supports, BLOCK), F32),
        ],
        compiler_params=pltpu.CompilerParams(vmem_limit_bytes=32 * MIB),
        name="make_tile",
    )(obs, noise, times, absorption, elimination, volume, weights)


def merge(mine, other, reps):
    peak_a, peak_b = mine[reps:], other[reps:]
    peak = jnp.maximum(peak_a, peak_b)
    scale_a, scale_b = jnp.exp(peak_a - peak)[:1], jnp.exp(peak_b - peak)[:1]
    return jnp.concatenate([mine[:reps] * scale_a + other[:reps] * scale_b, peak], axis=0)


def em_kernel(total_subjects, total_supports, ny, nz,
              obs_hbm, noise_hbm, times_hbm, absorption_hbm, elimination_hbm, volume_hbm, weights_hbm, counts_hbm,
              new_ref, loglik_ref,
              obs_v, noise_v, times_v, absorption_v, elimination_v, volume_v, weights_v, counts_v, load_sem,
              curves, current, linear_v, square_v, features_v, log_lik_even, log_lik_odd, tile, log_scale,
              mix_own, mix_start, mix_pair, mix_near, mix_far, factor,
              sums, y_in, z_out, z_in, held,
              mix_send, mix_recv, chunk_send, y_recv, z_recv, gz_recv, gy_recv):
    samples = obs_v.shape[0]
    all_reps, subjects = counts_v.shape
    reps = all_reps
    half = subjects // 2
    per_half = half // BLOCK
    supports = weights_v.shape[1]
    width = supports // CHUNKS
    piece_rows, piece = reps // nz, width // ny
    subj, supp = lax.axis_index("subj"), lax.axis_index("supp")
    y, z = lax.rem(subj, ny), lax.div(subj, ny)
    core = lax.rem(supp, 2)
    core_peer = {"subj": subj, "supp": supp + 1 - 2 * core}
    x_peer = {"subj": subj, "supp": lax.rem(supp + 2, 4)}
    y_peer = {"subj": subj + 1 - 2 * y, "supp": supp}
    z_at = [lax.rem(z + d, nz) for d in range(nz)]
    z_peers = [{"subj": z_at[d] * ny + y, "supp": supp} for d in range(nz)]
    in_flight = {}
    mix_rows = lambda it: all_reps + PEAK_ROWS if it == 0 else all_reps

    loads = [pltpu.make_async_copy(src, dst, load_sem.at[k]) for k, (src, dst) in enumerate((
        (absorption_hbm, absorption_v), (elimination_hbm, elimination_v), (volume_hbm, volume_v),
        (obs_hbm, obs_v), (noise_hbm, noise_v), (times_hbm, times_v), (weights_hbm, weights_v),
        (counts_hbm, counts_v)))]
    for load in loads:
        load.start()

    def send(src, dst, send_sem, recv_sem, peer, key):
        if key in in_flight:
            in_flight.pop(key)()
        copy = pltpu.make_async_remote_copy(
            src_ref=src, dst_ref=dst, send_sem=send_sem, recv_sem=recv_sem,
            device_id=peer, device_id_type=pl.DeviceIdType.MESH)
        copy.start()
        in_flight[key] = copy.wait_send
        return copy

    def send_chunk(src, dst, send_sem, recv_sem, peer, it, kind, every):
        if (it - 1, kind) in in_flight:
            in_flight.pop((it - 1, kind))()
        copy = pltpu.make_async_remote_copy(
            src_ref=src, dst_ref=dst, send_sem=send_sem, recv_sem=recv_sem,
            device_id=peer, device_id_type=pl.DeviceIdType.MESH)
        copy.start()
        in_flight[it, kind] = lambda: pltpu.make_async_copy(every, every, send_sem).wait()
        return copy

    def send_along_z(src_of, dst_of, send_sem, recv_sem, it, c, kind):
        for d in range(1, nz):
            send_chunk(src_of(d), dst_of(d), send_sem, recv_sem, z_peers[d], it, kind, z_in.at[it])
        return pltpu.make_async_copy(z_in.at[it, c], z_in.at[it, c], recv_sem)

    barrier = pltpu.get_barrier_semaphore()
    peers = [core_peer, x_peer, y_peer] + z_peers[1:]
    for peer in peers:
        pl.semaphore_signal(barrier, inc=1, device_id=peer, device_id_type=pl.DeviceIdType.MESH)

    for load in loads[:6]:
        load.wait()
    blocks = subjects // BLOCK
    starts = [pl.multiple_of((1 - core) * half + b * BLOCK, BLOCK) for b in range(per_half)]
    starts += [pl.multiple_of(core * half + b * BLOCK, BLOCK) for b in range(per_half)]
    columns = [pl.ds(at, BLOCK) for at in starts]
    offsets = {}

    def prepare(b):
        obs, noise = obs_v[:, columns[b]], noise_v[:, columns[b]]
        precision = 1.0 / (noise * noise)
        linear = obs * precision
        linear_v[...] = linear
        square_v[...] = -0.5 * precision
        offsets[b] = -0.5 * jnp.sum(obs * linear, axis=0, keepdims=True)
        scale = jnp.sum(jnp.log(noise), axis=0, keepdims=True)
        log_scale[:, columns[b]] = jnp.broadcast_to(scale, (PEAK_ROWS, BLOCK))

    def feature_rows(b, step):
        features = features_v.at[b % 2]
        for k in range(NT // FILL_STEPS // GROUP):
            first_row = pl.multiple_of(step * (NT // FILL_STEPS) + k * GROUP, GROUP)
            index = lax.broadcasted_iota(jnp.int32, (GROUP, BLOCK), 0) + first_row
            linear_part = jnp.zeros((GROUP, BLOCK), F32)
            square_part = jnp.zeros((GROUP, BLOCK), F32)
            for j in range(samples):
                hit = times_v[j:j + 1, columns[b]] == index
                linear_part = linear_part + jnp.where(hit, linear_v[j:j + 1, :], 0.0)
                square_part = square_part + jnp.where(hit, square_v[j:j + 1, :], 0.0)
            for base, part in ((0, linear_part), (NT, square_part)):
                hi, lo = split(part)
                for slot, value in ((0, hi), (1, lo), (2, hi)):
                    at = pl.ds(pl.multiple_of(slot * 2 * NT + base + first_row, GROUP), GROUP)
                    features[at, :] = value

    fill_step = supports // FILL_STEPS
    logs = (log_lik_even, log_lik_odd)

    prepare(0)

    curve_steps = supports // 512 // FILL_STEPS
    early = curve_steps // FILL_STEPS

    @pl.loop(0, FILL_STEPS)
    def _(step):
        for k in range(early):
            build_curves(absorption_v, elimination_v, volume_v, curves, step * early + k)
        feature_rows(0, step)

    for load in loads[6:]:
        load.wait()
    hi, lo = split(weights_v[...])
    current[...] = jnp.concatenate([hi, lo], axis=0)

    def fill_stage(b, peak_before):
        if b + 1 < blocks:
            prepare(b + 1)

        def one(step, carry):
            peak, mix = carry
            at = pl.ds(pl.multiple_of(step * fill_step, fill_step), fill_step)
            if b < blocks:
                part = jnp.dot(curves[at, :], features_v[b % 2], preferred_element_type=F32)
                logs[b % 2][at, :] = part
                peak = jnp.maximum(peak, jnp.max(part.reshape(fill_step // 8, 8, BLOCK), axis=0))
            if b > 0:
                like = jnp.exp(logs[(b - 1) % 2][at, :] - peak_before).astype(BF16)
                tile[at, columns[b - 1]] = like
                mix = mix + jnp.dot(current[:, at], like, preferred_element_type=F32)
            if b + 1 < blocks:
                feature_rows(b + 1, step)
            return peak, mix

        peak, mix = jnp.full((8, BLOCK), -jnp.inf, F32), jnp.zeros((2 * all_reps, BLOCK), F32)
        if b == 0:
            peak, mix = one(0, (peak, mix))
            for k in range(curve_steps, FILL_STEPS * curve_steps):
                build_curves(absorption_v, elimination_v, volume_v, curves, k)
            later = lambda carry: lax.fori_loop(1, FILL_STEPS, one, carry)
            peak, mix = lax.cond(core < 2, later, lambda carry: carry, (peak, mix))
        else:
            peak, mix = lax.fori_loop(0, FILL_STEPS, one, (peak, mix))
        if b > 0:
            side = 1 - core if b - 1 < per_half else core
            within = slice((b - 1) % per_half * BLOCK, ((b - 1) % per_half + 1) * BLOCK)
            mix = mix[:all_reps] + mix[all_reps:]
            mix_start[0, side, :all_reps, within] = mix
            mix_start[0, side, all_reps:, within] = jnp.broadcast_to(
                peak_before + offsets[b - 1], (PEAK_ROWS, BLOCK))
        return jnp.max(peak, axis=0, keepdims=True)

    first = {}

    def start_exchange(it):
        to_send = pl.ds(0, mix_rows(it))
        first[it] = send(mix_start.at[it, 1 - core, to_send], mix_near.at[it, to_send], mix_send.at[0],
                         mix_recv.at[0], core_peer, ("mix", 0))

    def stages_of(it):
        mixed = pl.ds(0, mix_rows(it))
        join = (lambda a, b: merge(a, b, reps)) if it == 0 else (lambda a, b: a + b)
        live = {}
        x_copies, core_copies, y_copies, z_copies, gz_copies, gy_copies = {}, {}, {}, {}, {}, {}

        def to_x(p):
            within = pl.ds(p * BLOCK, BLOCK)
            if p == 0:
                first[it].wait_recv()
            pair = mix_pair.at[it, mixed, within]
            pair[...] = join(mix_start[it, core, mixed, within], mix_near[it, mixed, within])
            at = 1 + per_half * (1 + it) + p
            x_copies[p] = send(pair, mix_far.at[it, mixed, within], mix_send.at[at], mix_recv.at[at], x_peer, ("mix", at))

        def to_core(p):
            within = pl.ds(p * BLOCK, BLOCK)
            x_copies[p].wait_recv()
            own = mix_own.at[it, core, mixed, within]
            own[...] = join(mix_pair[it, mixed, within], mix_far[it, mixed, within])
            core_copies[p] = send(own, own, mix_send.at[1 + p], mix_recv.at[1 + p], core_peer, ("mix", 1 + p))

        def respond():
            for copy in core_copies.values():
                copy.wait_recv()
            parts = []
            for side in range(2):
                columns = slice(side * half, (side + 1) * half)
                mixture = mix_own[it, side, :reps, :]
                if it == 0:
                    peak = mix_own[0, side, reps:, :]
                    factor[:, columns] = jnp.exp(mix_start[0, side, reps:, :] - peak)
                    loglik_ref[:, columns] = (
                        peak[:1] + jnp.log(mixture / total_supports) - log_scale[:1, columns]
                    ) / samples - 0.5 * math.log(2.0 * math.pi)
                counts = counts_v[:, columns]
                drawn = counts > 0
                resp = jnp.where(drawn, counts.astype(F32) / jnp.where(drawn, mixture, 1.0), 0.0)
                parts.append(resp * factor[:1, columns])
            hi, lo = split(jnp.concatenate(parts, axis=1))
            live["resp"] = jnp.concatenate([hi, lo], axis=0)

        def compute(c):
            both = lax.dot_general(live["resp"], tile[c * width:(c + 1) * width, :],
                                   (((1,), (1,)), ((), ())), preferred_element_type=F32)
            part = both[:reps] + both[reps:]
            for a in range(ny):
                for b in range(nz):
                    sums[it, c, a, b] = part[b * piece_rows:(b + 1) * piece_rows, a * piece:(a + 1) * piece]
            y_copies[c] = send_chunk(sums.at[it, c, 1 - y], y_in.at[it, c], chunk_send.at[0],
                                     y_recv.at[c], y_peer, it, "y", y_in.at[it])

        def over_z(c):
            y_copies[c].wait_recv()
            z_out[it, c] = sums[it, c, y] + y_in[it, c]
            z_copies[c] = send_along_z(lambda d: z_out.at[it, c, z_at[d]], lambda d: z_in.at[it, c, d - 1],
                                       chunk_send.at[1], z_recv.at[c], it, c, "z")

        def update(c):
            total = z_out[it, c, z]
            z_copies[c].wait()
            for d in range(1, nz):
                total = total + z_in[it, c, d - 1]
            if it == 0:
                rows = pl.ds(pl.multiple_of(z * piece_rows, piece_rows), piece_rows)
                before = weights_v[rows, pl.ds(pl.multiple_of(c * width + y * piece, piece), piece)]
            else:
                before = held[it - 1, c, y, z]
            held[it, c, y, z] = before * total / total_subjects
            gz_copies[c] = send_along_z(lambda d: held.at[it, c, y, z], lambda d: held.at[it, c, y, z],
                                        chunk_send.at[2], gz_recv.at[c], it, c, "gz")

        def over_y(c):
            gz_copies[c].wait()
            gy_copies[c] = send_chunk(held.at[it, c, y], held.at[it, c, y], chunk_send.at[3],
                                      gy_recv.at[c], y_peer, it, "gy", y_in.at[it])

        def finish(c):
            gy_copies[c].wait_recv()
            now = jnp.concatenate([held[it, c, a].reshape(reps, piece) for a in range(ny)], axis=1)
            if it == ITERS - 1:
                new_ref[:, c * width:(c + 1) * width] = now
                return
            hi, lo = split(now)
            both = jnp.concatenate([hi, lo], axis=0)
            for side in (1 - core, core):
                at = pl.ds(pl.multiple_of(side * half, half), half)
                part = jnp.dot(both, tile[c * width:(c + 1) * width, at], preferred_element_type=F32)
                key = "mix_own" if side is core else "mix_other"
                live[key] = part if c == 0 else live[key] + part
                if c == CHUNKS - 1:
                    mix_start[it + 1, side, :reps, :] = (live[key][:reps] + live[key][reps:]) * factor[:1, at]
                    if side is not core:
                        start_exchange(it + 1)

        order = [(PACE * c, c, functools.partial(compute, c)) for c in range(CHUNKS)]
        order += [(c + late, c, functools.partial(stage, c)) for c in range(CHUNKS)
                  for late, stage in zip(LATE, (over_z, update, over_y, finish))]
        halves = range(per_half)
        return ([functools.partial(to_x, p) for p in halves], [functools.partial(to_core, p) for p in halves]
                + [respond] + [stage for _, _, stage in sorted(order, key=lambda entry: entry[:2])])

    peak = None
    for it in range(ITERS):
        sends, rest = stages_of(it)
        if it == 0:
            for b in range(blocks + 1):
                peak = fill_stage(b, peak)
                if b == per_half:
                    pl.semaphore_wait(barrier, len(peers))
                    start_exchange(0)
                if b > per_half:
                    sends[b - 1 - per_half]()
            sends = []
        for stage in sends + rest:
            stage()
    for wait in in_flight.values():
        wait()


def run_em(obs, noise, times, absorption, elimination, volume, weights, counts, ny, nz, sizes):
    reps, supports = weights.shape
    samples, subjects = obs.shape
    half = subjects // 2
    piece = (reps // nz, supports // (CHUNKS * ny))
    rows = reps + PEAK_ROWS
    dma = lambda *shape: pltpu.SemaphoreType.DMA(shape)
    vmem = lambda *shape: pltpu.VMEM(shape, F32)
    parts = (ITERS, CHUNKS)
    inputs = (obs, noise, times, absorption, elimination, volume, weights, counts)
    return pl.pallas_call(
        functools.partial(em_kernel, float(sizes[0]), float(sizes[1]), ny, nz),
        out_shape=[pltpu.VMEM((reps, supports), F32), pltpu.VMEM((reps, subjects), F32)],
        in_specs=[pl.BlockSpec(memory_space=pltpu.HBM)] * len(inputs),
        out_specs=[pl.BlockSpec(memory_space=pltpu.VMEM)] * 2,
        scratch_shapes=[pltpu.VMEM(a.shape, a.dtype) for a in inputs] + [
            dma(len(inputs)),
            pltpu.VMEM((supports, 6 * NT), BF16), pltpu.VMEM((2 * reps, supports), BF16),
            vmem(samples, BLOCK), vmem(samples, BLOCK), pltpu.VMEM((2, 6 * NT, BLOCK), BF16),
            vmem(supports, BLOCK), vmem(supports, BLOCK), pltpu.VMEM((supports, subjects), BF16),
            vmem(PEAK_ROWS, subjects),
            vmem(ITERS, 2, rows, half), vmem(ITERS, 2, rows, half), vmem(ITERS, rows, half),
            vmem(ITERS, rows, half), vmem(ITERS, rows, half), vmem(PEAK_ROWS, subjects),
            vmem(*parts, ny, nz, *piece), vmem(*parts, nz, *piece),
            vmem(*parts, nz, *piece), vmem(*parts, nz - 1, *piece),
            vmem(*parts, ny, nz, *piece),
            *[dma(1 + (1 + ITERS) * (half // BLOCK))] * 2, dma(4), *[dma(CHUNKS)] * 4,
        ],
        compiler_params=pltpu.CompilerParams(collective_id=0, has_side_effects=True, vmem_limit_bytes=56 * MIB),
        name="em_steps",
    )(*inputs)


def hand_over(new, loglik):
    rows = 8

    def kernel(new_in, loglik_in, new_out, loglik_out, sem):
        copies = [pltpu.make_async_copy(new_in.at[pl.ds(k * rows, rows)], new_out.at[pl.ds(k * rows, rows)], sem.at[k])
                  for k in range(new_in.shape[0] // rows)]
        copies.append(pltpu.make_async_copy(loglik_in, loglik_out, sem.at[len(copies)]))
        for copy in copies:
            copy.start()
        for copy in copies:
            copy.wait()

    return pl.pallas_call(
        kernel,
        out_shape=[jax.ShapeDtypeStruct(new.shape, F32), jax.ShapeDtypeStruct(loglik.shape, F32)],
        in_specs=[pl.BlockSpec(memory_space=pltpu.VMEM)] * 2,
        out_specs=[pl.BlockSpec(memory_space=pltpu.HBM)] * 2,
        scratch_shapes=[pltpu.SemaphoreType.DMA((1 + new.shape[0] // rows,))],
        name="hand_over",
    )(new, loglik)


def plain_em(tile, mix, log_scale, counts, weights, samples, total_subjects, total_supports):
    reps = weights.shape[0]
    both = jnp.concatenate([mix[0], mix[1]], axis=1)
    local_peak = both[reps]
    peak = lax.pmax(local_peak, "supp")
    factor = jnp.exp(local_peak - peak)
    partial_mix = both[:reps]
    drawn = counts > 0
    current = weights
    loglik = None
    for it in range(ITERS):
        if it > 0:
            hi, lo = split(current)
            pair = jnp.dot(jnp.concatenate([hi, lo], axis=0), tile, preferred_element_type=F32)
            partial_mix = pair[:reps] + pair[reps:]
        mixture = lax.psum(partial_mix * factor, "supp")
        if it == 0:
            loglik = (peak + jnp.log(mixture / total_supports) - log_scale[:1]) / samples
            loglik = loglik - 0.5 * math.log(2.0 * math.pi)
        resp = jnp.where(drawn, counts.astype(F32) / jnp.where(drawn, mixture, 1.0), 0.0) * factor
        hi, lo = split(resp)
        pair = lax.dot_general(jnp.concatenate([hi, lo], axis=0), tile, (((1,), (1,)), ((), ())),
                               preferred_element_type=F32)
        current = current * lax.psum(pair[:reps] + pair[reps:], "subj") / total_subjects
    return current, loglik


def body(observations, noise_scale, sample_times, counts, absorption, elimination, volume, weights):
    n_subj, n_supp = lax.axis_size("subj"), lax.axis_size("supp")
    subjects, samples = observations.shape
    sizes = (subjects * n_subj, weights.shape[1] * n_supp)
    inputs = (observations.T, noise_scale.T, sample_times.T,
              absorption[None, :], elimination[None, :], volume[None, :], weights)
    if (n_subj, n_supp) == (8, 4):
        new, loglik = run_em(*inputs, counts, 2, 4, sizes)
        return hand_over(pltpu.with_memory_space_constraint(new, pltpu.VMEM), pltpu.with_memory_space_constraint(loglik, pltpu.VMEM))
    return plain_em(*make_tile(*inputs), counts, weights, samples, *sizes)


def solution(mesh):
    return jax.shard_map(
        body,
        mesh=mesh,
        in_specs=(
            P("subj", None),
            P("subj", None),
            P("subj", None),
            P(None, "subj"),
            P("supp"),
            P("supp"),
            P("supp"),
            P(None, "supp"),
        ),
        out_specs=(P(None, "supp"), P(None, "subj")),
        check_vma=False,
    )
```

```python
import functools
import math

import jax
import jax.numpy as jnp
from jax import lax
from jax.experimental import pallas as pl
from jax.experimental.pallas import tpu as pltpu
from jax.sharding import PartitionSpec as P

NT = 128
HORIZON = 24.0
ITERS = 2
BLOCK = 256
KSTEP = 2048
CHUNKS = 8
FILL_STEPS = 2
GROUP = 32
PEAK_ROWS = 8
LATE = (3.2, 10.7, 18.2, 25.7)
PACE = 0.62
MIB = 1 << 20
F32 = jnp.float32
BF16 = jnp.bfloat16


def split(x):
    hi = x.astype(BF16)
    return hi, (x - hi.astype(F32)).astype(BF16)


def build_curves(absorption_ref, elimination_ref, volume_ref, curves, step):
    step_size = 512
    grid_rows = lax.broadcasted_iota(jnp.int32, (NT, step_size), 0).astype(F32)
    time_grid = (grid_rows + 1.0) * (HORIZON / NT)

    at = pl.ds(pl.multiple_of(step * step_size, step_size), step_size)
    rate_in = absorption_ref[:, at]
    rate_out = elimination_ref[:, at]
    amplitude = rate_in / (volume_ref[:, at] * (rate_in - rate_out))
    rows = amplitude * (jnp.exp(-rate_out * time_grid) - jnp.exp(-rate_in * time_grid))
    columns = rows.T
    for half, part in ((0, columns), (NT, columns * columns)):
        hi, lo = split(part)
        curves[at, half:half + NT] = hi
        curves[at, 2 * NT + half:3 * NT + half] = hi
        curves[at, 4 * NT + half:5 * NT + half] = lo


def block_mixture(obs, noise, times, curves, current, log_lik, tile_ref, columns):
    supports = log_lik.shape[0]
    steps = supports // KSTEP
    precision = 1.0 / (noise * noise)
    linear = obs * precision
    square = -0.5 * precision
    grid_index = lax.broadcasted_iota(jnp.int32, (NT, BLOCK), 0)
    linear_part = jnp.zeros((NT, BLOCK), F32)
    square_part = jnp.zeros((NT, BLOCK), F32)
    for j in range(obs.shape[0]):
        hit = times[j:j + 1, :] == grid_index
        linear_part = linear_part + jnp.where(hit, linear[j:j + 1, :], 0.0)
        square_part = square_part + jnp.where(hit, square[j:j + 1, :], 0.0)
    offset = -0.5 * jnp.sum(obs * obs * precision, axis=0, keepdims=True)
    log_scale = jnp.sum(jnp.log(noise), axis=0, keepdims=True)
    hi, lo = split(jnp.concatenate([linear_part, square_part], axis=0))
    features = jnp.concatenate([hi, lo, hi], axis=0)

    def one_log(step, peak):
        at = pl.ds(pl.multiple_of(step * KSTEP, KSTEP), KSTEP)
        part = jnp.dot(curves[at, :], features, preferred_element_type=F32)
        log_lik[at, :] = part
        return jnp.maximum(peak, jnp.max(part.reshape(KSTEP // 8, 8, BLOCK), axis=0))

    peak = lax.fori_loop(0, steps, one_log, jnp.full((8, BLOCK), -jnp.inf, F32))
    peak = jnp.max(peak, axis=0, keepdims=True)

    def one_tile(step, mix):
        at = pl.ds(pl.multiple_of(step * KSTEP, KSTEP), KSTEP)
        like = jnp.exp(log_lik[at, :] - peak).astype(BF16)
        tile_ref[at, columns] = like
        return mix + jnp.dot(current[:, at], like, preferred_element_type=F32)

    mix = lax.fori_loop(0, steps, one_tile, jnp.zeros((current.shape[0], BLOCK), F32))
    return mix, peak + offset, log_scale


def tile_kernel(obs_ref, noise_ref, times_ref, absorption_ref, elimination_ref, volume_ref,
                weights_ref, tile_ref, mix_ref, scale_ref, curves, current, log_lik):
    reps = weights_ref.shape[0]

    @pl.when(pl.program_id(0) == 0)
    def _():
        hi, lo = split(weights_ref[...])
        current[...] = jnp.concatenate([hi, lo], axis=0)
        @pl.loop(0, absorption_ref.shape[1] // 512)
        def _(step):
            build_curves(absorption_ref, elimination_ref, volume_ref, curves, step)

    mix, peak, log_scale = block_mixture(obs_ref[...], noise_ref[...], times_ref[...], curves, current,
                                         log_lik, tile_ref, slice(None))
    mix_ref[0, :reps, :] = mix[:reps] + mix[reps:]
    mix_ref[0, reps:, :] = jnp.broadcast_to(peak, (PEAK_ROWS, BLOCK))
    scale_ref[...] = jnp.broadcast_to(log_scale, (PEAK_ROWS, BLOCK))


def make_tile(obs, noise, times, absorption, elimination, volume, weights):
    samples, subjects = obs.shape
    reps, supports = weights.shape
    half = subjects // 2
    per_half = half // BLOCK
    by_subject = pl.BlockSpec((samples, BLOCK), lambda b: (0, b))
    whole = lambda shape: pl.BlockSpec(shape, lambda b: (0, 0))
    return pl.pallas_call(
        tile_kernel,
        grid=(subjects // BLOCK,),
        in_specs=[by_subject] * 3 + [whole((1, supports))] * 3 + [whole((reps, supports))],
        out_specs=[
            pl.BlockSpec((supports, BLOCK), lambda b: (0, b)),
            pl.BlockSpec((1, reps + PEAK_ROWS, BLOCK), lambda b: (b // per_half, 0, b % per_half)),
            pl.BlockSpec((PEAK_ROWS, BLOCK), lambda b: (0, b)),
        ],
        out_shape=[
            jax.ShapeDtypeStruct((supports, subjects), BF16),
            jax.ShapeDtypeStruct((2, reps + PEAK_ROWS, half), F32),
            jax.ShapeDtypeStruct((PEAK_ROWS, subjects), F32),
        ],
        scratch_shapes=[
            pltpu.VMEM((supports, 6 * NT), BF16),
            pltpu.VMEM((2 * reps, supports), BF16),
            pltpu.VMEM((supports, BLOCK), F32),
        ],
        compiler_params=pltpu.CompilerParams(vmem_limit_bytes=32 * MIB),
        name="make_tile",
    )(obs, noise, times, absorption, elimination, volume, weights)


def merge(mine, other, reps):
    peak_a, peak_b = mine[reps:], other[reps:]
    peak = jnp.maximum(peak_a, peak_b)
    scale_a, scale_b = jnp.exp(peak_a - peak)[:1], jnp.exp(peak_b - peak)[:1]
    return jnp.concatenate([mine[:reps] * scale_a + other[:reps] * scale_b, peak], axis=0)


def em_kernel(total_subjects, total_supports, ny, nz,
              obs_hbm, noise_hbm, times_hbm, absorption_hbm, elimination_hbm, volume_hbm, weights_hbm, counts_hbm,
              new_ref, loglik_ref,
              obs_v, noise_v, times_v, absorption_v, elimination_v, volume_v, weights_v, counts_v, load_sem,
              curves, current, linear_v, square_v, features_v, log_lik_even, log_lik_odd, tile, log_scale,
              mix_own, mix_start, mix_pair, mix_near, mix_far, factor,
              sums, y_in, z_out, z_in, held,
              mix_send, mix_recv, chunk_send, y_recv, z_recv, gz_recv, gy_recv):
    samples = obs_v.shape[0]
    all_reps, subjects = counts_v.shape
    reps = all_reps
    half = subjects // 2
    per_half = half // BLOCK
    supports = weights_v.shape[1]
    width = supports // CHUNKS
    piece_rows, piece = reps // nz, width // ny
    subj, supp = lax.axis_index("subj"), lax.axis_index("supp")
    y, z = lax.rem(subj, ny), lax.div(subj, ny)
    core = lax.rem(supp, 2)
    core_peer = {"subj": subj, "supp": supp + 1 - 2 * core}
    x_peer = {"subj": subj, "supp": lax.rem(supp + 2, 4)}
    y_peer = {"subj": subj + 1 - 2 * y, "supp": supp}
    z_at = [lax.rem(z + d, nz) for d in range(nz)]
    z_peers = [{"subj": z_at[d] * ny + y, "supp": supp} for d in range(nz)]
    in_flight = {}
    mix_rows = lambda it: all_reps + PEAK_ROWS if it == 0 else all_reps

    loads = [pltpu.make_async_copy(src, dst, load_sem.at[k]) for k, (src, dst) in enumerate((
        (absorption_hbm, absorption_v), (elimination_hbm, elimination_v), (volume_hbm, volume_v),
        (obs_hbm, obs_v), (noise_hbm, noise_v), (times_hbm, times_v), (weights_hbm, weights_v),
        (counts_hbm, counts_v)))]
    for load in loads:
        load.start()

    def send(src, dst, send_sem, recv_sem, peer, key):
        if key in in_flight:
            in_flight.pop(key)()
        copy = pltpu.make_async_remote_copy(
            src_ref=src, dst_ref=dst, send_sem=send_sem, recv_sem=recv_sem,
            device_id=peer, device_id_type=pl.DeviceIdType.MESH)
        copy.start()
        in_flight[key] = copy.wait_send
        return copy

    def send_chunk(src, dst, send_sem, recv_sem, peer, it, kind, every):
        if (it - 1, kind) in in_flight:
            in_flight.pop((it - 1, kind))()
        copy = pltpu.make_async_remote_copy(
            src_ref=src, dst_ref=dst, send_sem=send_sem, recv_sem=recv_sem,
            device_id=peer, device_id_type=pl.DeviceIdType.MESH)
        copy.start()
        in_flight[it, kind] = lambda: pltpu.make_async_copy(every, every, send_sem).wait()
        return copy

    def send_along_z(src_of, dst_of, send_sem, recv_sem, it, c, kind):
        for d in range(1, nz):
            send_chunk(src_of(d), dst_of(d), send_sem, recv_sem, z_peers[d], it, kind, z_in.at[it])
        return pltpu.make_async_copy(z_in.at[it, c], z_in.at[it, c], recv_sem)

    barrier = pltpu.get_barrier_semaphore()
    peers = [core_peer, x_peer, y_peer] + z_peers[1:]
    for peer in peers:
        pl.semaphore_signal(barrier, inc=1, device_id=peer, device_id_type=pl.DeviceIdType.MESH)

    for load in loads[:6]:
        load.wait()
    blocks = subjects // BLOCK
    starts = [pl.multiple_of((1 - core) * half + b * BLOCK, BLOCK) for b in range(per_half)]
    starts += [pl.multiple_of(core * half + b * BLOCK, BLOCK) for b in range(per_half)]
    columns = [pl.ds(at, BLOCK) for at in starts]
    offsets = {}

    def prepare(b):
        obs, noise = obs_v[:, columns[b]], noise_v[:, columns[b]]
        precision = 1.0 / (noise * noise)
        linear = obs * precision
        linear_v[...] = linear
        square_v[...] = -0.5 * precision
        offsets[b] = -0.5 * jnp.sum(obs * linear, axis=0, keepdims=True)
        scale = jnp.sum(jnp.log(noise), axis=0, keepdims=True)
        log_scale[:, columns[b]] = jnp.broadcast_to(scale, (PEAK_ROWS, BLOCK))

    def feature_rows(b, step):
        features = features_v.at[b % 2]
        for k in range(NT // FILL_STEPS // GROUP):
            first_row = pl.multiple_of(step * (NT // FILL_STEPS) + k * GROUP, GROUP)
            index = lax.broadcasted_iota(jnp.int32, (GROUP, BLOCK), 0) + first_row
            linear_part = jnp.zeros((GROUP, BLOCK), F32)
            square_part = jnp.zeros((GROUP, BLOCK), F32)
            for j in range(samples):
                hit = times_v[j:j + 1, columns[b]] == index
                linear_part = linear_part + jnp.where(hit, linear_v[j:j + 1, :], 0.0)
                square_part = square_part + jnp.where(hit, square_v[j:j + 1, :], 0.0)
            for base, part in ((0, linear_part), (NT, square_part)):
                hi, lo = split(part)
                for slot, value in ((0, hi), (1, lo), (2, hi)):
                    at = pl.ds(pl.multiple_of(slot * 2 * NT + base + first_row, GROUP), GROUP)
                    features[at, :] = value

    fill_step = supports // FILL_STEPS
    logs = (log_lik_even, log_lik_odd)

    prepare(0)

    curve_steps = supports // 512 // FILL_STEPS
    early = curve_steps // FILL_STEPS

    @pl.loop(0, FILL_STEPS)
    def _(step):
        for k in range(early):
            build_curves(absorption_v, elimination_v, volume_v, curves, step * early + k)
        feature_rows(0, step)

    for load in loads[6:]:
        load.wait()
    hi, lo = split(weights_v[...])
    current[...] = jnp.concatenate([hi, lo], axis=0)

    def fill_stage(b, peak_before):
        if b + 1 < blocks:
            prepare(b + 1)

        last = b == blocks
        span = supports if last else fill_step

        def one(step, carry):
            peak, mix = carry
            at = pl.ds(pl.multiple_of(step * span, span), span)
            if b < blocks:
                part = jnp.dot(curves[at, :], features_v[b % 2], preferred_element_type=F32)
                logs[b % 2][at, :] = part
                peak = jnp.maximum(peak, jnp.max(part.reshape(fill_step // 8, 8, BLOCK), axis=0))
            if b > 0:
                like = jnp.exp(logs[(b - 1) % 2][at, :] - peak_before).astype(BF16)
                tile[at, columns[b - 1]] = like
                mix = mix + jnp.dot(current[:, at], like, preferred_element_type=F32)
            if b + 1 < blocks:
                feature_rows(b + 1, step)
            return peak, mix

        peak, mix = jnp.full((8, BLOCK), -jnp.inf, F32), jnp.zeros((2 * all_reps, BLOCK), F32)
        if b == 0:
            peak, mix = one(0, (peak, mix))
            for k in range(curve_steps, FILL_STEPS * curve_steps):
                build_curves(absorption_v, elimination_v, volume_v, curves, k)
            later = lambda carry: lax.fori_loop(1, FILL_STEPS, one, carry)
            peak, mix = lax.cond(core < 2, later, lambda carry: carry, (peak, mix))
        else:
            peak, mix = lax.fori_loop(0, 1 if last else FILL_STEPS, one, (peak, mix))
        if b > 0:
            side = 1 - core if b - 1 < per_half else core
            within = slice((b - 1) % per_half * BLOCK, ((b - 1) % per_half + 1) * BLOCK)
            mix = mix[:all_reps] + mix[all_reps:]
            mix_start[0, side, :all_reps, within] = mix
            mix_start[0, side, all_reps:, within] = jnp.broadcast_to(
                peak_before + offsets[b - 1], (PEAK_ROWS, BLOCK))
        return jnp.max(peak, axis=0, keepdims=True)

    first = {}

    def start_exchange(it):
        to_send = pl.ds(0, mix_rows(it))
        first[it] = send(mix_start.at[it, 1 - core, to_send], mix_near.at[it, to_send], mix_send.at[0],
                         mix_recv.at[0], core_peer, ("mix", 0))

    def stages_of(it):
        mixed = pl.ds(0, mix_rows(it))
        join = (lambda a, b: merge(a, b, reps)) if it == 0 else (lambda a, b: a + b)
        live = {}
        x_copies, core_copies, y_copies, z_copies, gz_copies, gy_copies = {}, {}, {}, {}, {}, {}

        def to_x(p):
            within = pl.ds(p * BLOCK, BLOCK)
            if p == 0:
                first[it].wait_recv()
            pair = mix_pair.at[it, mixed, within]
            pair[...] = join(mix_start[it, core, mixed, within], mix_near[it, mixed, within])
            at = 1 + per_half * (1 + it) + p
            x_copies[p] = send(pair, mix_far.at[it, mixed, within], mix_send.at[at], mix_recv.at[at], x_peer, ("mix", at))

        def to_core(p):
            within = pl.ds(p * BLOCK, BLOCK)
            x_copies[p].wait_recv()
            own = mix_own.at[it, core, mixed, within]
            own[...] = join(mix_pair[it, mixed, within], mix_far[it, mixed, within])
            core_copies[p] = send(own, own, mix_send.at[1 + p], mix_recv.at[1 + p], core_peer, ("mix", 1 + p))

        def respond():
            for copy in core_copies.values():
                copy.wait_recv()
            parts = []
            for side in range(2):
                columns = slice(side * half, (side + 1) * half)
                mixture = mix_own[it, side, :reps, :]
                if it == 0:
                    peak = mix_own[0, side, reps:, :]
                    factor[:, columns] = jnp.exp(mix_start[0, side, reps:, :] - peak)
                    loglik_ref[:, columns] = (
                        peak[:1] + jnp.log(mixture / total_supports) - log_scale[:1, columns]
                    ) / samples - 0.5 * math.log(2.0 * math.pi)
                counts = counts_v[:, columns]
                drawn = counts > 0
                resp = jnp.where(drawn, counts.astype(F32) / jnp.where(drawn, mixture, 1.0), 0.0)
                parts.append(resp * factor[:1, columns])
            hi, lo = split(jnp.concatenate(parts, axis=1))
            live["resp"] = jnp.concatenate([hi, lo], axis=0)

        def compute(c):
            both = lax.dot_general(live["resp"], tile[c * width:(c + 1) * width, :],
                                   (((1,), (1,)), ((), ())), preferred_element_type=F32)
            part = both[:reps] + both[reps:]
            for a in range(ny):
                for b in range(nz):
                    sums[it, c, a, b] = part[b * piece_rows:(b + 1) * piece_rows, a * piece:(a + 1) * piece]
            y_copies[c] = send_chunk(sums.at[it, c, 1 - y], y_in.at[it, c], chunk_send.at[0],
                                     y_recv.at[c], y_peer, it, "y", y_in.at[it])

        def over_z(c):
            y_copies[c].wait_recv()
            z_out[it, c] = sums[it, c, y] + y_in[it, c]
            z_copies[c] = send_along_z(lambda d: z_out.at[it, c, z_at[d]], lambda d: z_in.at[it, c, d - 1],
                                       chunk_send.at[1], z_recv.at[c], it, c, "z")

        def update(c):
            total = z_out[it, c, z]
            z_copies[c].wait()
            for d in range(1, nz):
                total = total + z_in[it, c, d - 1]
            if it == 0:
                rows = pl.ds(pl.multiple_of(z * piece_rows, piece_rows), piece_rows)
                before = weights_v[rows, pl.ds(pl.multiple_of(c * width + y * piece, piece), piece)]
            else:
                before = held[it - 1, c, y, z]
            held[it, c, y, z] = before * total / total_subjects
            gz_copies[c] = send_along_z(lambda d: held.at[it, c, y, z], lambda d: held.at[it, c, y, z],
                                        chunk_send.at[2], gz_recv.at[c], it, c, "gz")

        def over_y(c):
            gz_copies[c].wait()
            gy_copies[c] = send_chunk(held.at[it, c, y], held.at[it, c, y], chunk_send.at[3],
                                      gy_recv.at[c], y_peer, it, "gy", y_in.at[it])

        def finish(c):
            gy_copies[c].wait_recv()
            now = jnp.concatenate([held[it, c, a].reshape(reps, piece) for a in range(ny)], axis=1)
            if it == ITERS - 1:
                new_ref[:, c * width:(c + 1) * width] = now
                return
            hi, lo = split(now)
            both = jnp.concatenate([hi, lo], axis=0)
            for side in (1 - core, core):
                at = pl.ds(pl.multiple_of(side * half, half), half)
                part = jnp.dot(both, tile[c * width:(c + 1) * width, at], preferred_element_type=F32)
                key = "mix_own" if side is core else "mix_other"
                live[key] = part if c == 0 else live[key] + part
                if c == CHUNKS - 1:
                    mix_start[it + 1, side, :reps, :] = (live[key][:reps] + live[key][reps:]) * factor[:1, at]
                    if side is not core:
                        start_exchange(it + 1)

        order = [(PACE * c, c, functools.partial(compute, c)) for c in range(CHUNKS)]
        order += [(c + late, c, functools.partial(stage, c)) for c in range(CHUNKS)
                  for late, stage in zip(LATE, (over_z, update, over_y, finish))]
        halves = range(per_half)
        return ([functools.partial(to_x, p) for p in halves], [functools.partial(to_core, p) for p in halves]
                + [respond] + [stage for _, _, stage in sorted(order, key=lambda entry: entry[:2])])

    peak = None
    for it in range(ITERS):
        sends, rest = stages_of(it)
        if it == 0:
            for b in range(blocks + 1):
                peak = fill_stage(b, peak)
                if b == per_half:
                    pl.semaphore_wait(barrier, len(peers))
                    start_exchange(0)
                if b > per_half:
                    sends[b - 1 - per_half]()
            sends = []
        for stage in sends + rest:
            stage()
    for wait in in_flight.values():
        wait()


def run_em(obs, noise, times, absorption, elimination, volume, weights, counts, ny, nz, sizes):
    reps, supports = weights.shape
    samples, subjects = obs.shape
    half = subjects // 2
    piece = (reps // nz, supports // (CHUNKS * ny))
    rows = reps + PEAK_ROWS
    dma = lambda *shape: pltpu.SemaphoreType.DMA(shape)
    vmem = lambda *shape: pltpu.VMEM(shape, F32)
    parts = (ITERS, CHUNKS)
    inputs = (obs, noise, times, absorption, elimination, volume, weights, counts)
    return pl.pallas_call(
        functools.partial(em_kernel, float(sizes[0]), float(sizes[1]), ny, nz),
        out_shape=[pltpu.VMEM((reps, supports), F32), pltpu.VMEM((reps, subjects), F32)],
        in_specs=[pl.BlockSpec(memory_space=pltpu.HBM)] * len(inputs),
        out_specs=[pl.BlockSpec(memory_space=pltpu.VMEM)] * 2,
        scratch_shapes=[pltpu.VMEM(a.shape, a.dtype) for a in inputs] + [
            dma(len(inputs)),
            pltpu.VMEM((supports, 6 * NT), BF16), pltpu.VMEM((2 * reps, supports), BF16),
            vmem(samples, BLOCK), vmem(samples, BLOCK), pltpu.VMEM((2, 6 * NT, BLOCK), BF16),
            vmem(supports, BLOCK), vmem(supports, BLOCK), pltpu.VMEM((supports, subjects), BF16),
            vmem(PEAK_ROWS, subjects),
            vmem(ITERS, 2, rows, half), vmem(ITERS, 2, rows, half), vmem(ITERS, rows, half),
            vmem(ITERS, rows, half), vmem(ITERS, rows, half), vmem(PEAK_ROWS, subjects),
            vmem(*parts, ny, nz, *piece), vmem(*parts, nz, *piece),
            vmem(*parts, nz, *piece), vmem(*parts, nz - 1, *piece),
            vmem(*parts, ny, nz, *piece),
            *[dma(1 + (1 + ITERS) * (half // BLOCK))] * 2, dma(4), *[dma(CHUNKS)] * 4,
        ],
        compiler_params=pltpu.CompilerParams(collective_id=0, has_side_effects=True, vmem_limit_bytes=56 * MIB),
        name="em_steps",
    )(*inputs)


def hand_over(new, loglik):
    rows = 8

    def kernel(new_in, loglik_in, new_out, loglik_out, sem):
        copies = [pltpu.make_async_copy(new_in.at[pl.ds(k * rows, rows)], new_out.at[pl.ds(k * rows, rows)], sem.at[k])
                  for k in range(new_in.shape[0] // rows)]
        copies.append(pltpu.make_async_copy(loglik_in, loglik_out, sem.at[len(copies)]))
        for copy in copies:
            copy.start()
        for copy in copies:
            copy.wait()

    return pl.pallas_call(
        kernel,
        out_shape=[jax.ShapeDtypeStruct(new.shape, F32), jax.ShapeDtypeStruct(loglik.shape, F32)],
        in_specs=[pl.BlockSpec(memory_space=pltpu.VMEM)] * 2,
        out_specs=[pl.BlockSpec(memory_space=pltpu.HBM)] * 2,
        scratch_shapes=[pltpu.SemaphoreType.DMA((1 + new.shape[0] // rows,))],
        name="hand_over",
    )(new, loglik)


def plain_em(tile, mix, log_scale, counts, weights, samples, total_subjects, total_supports):
    reps = weights.shape[0]
    both = jnp.concatenate([mix[0], mix[1]], axis=1)
    local_peak = both[reps]
    peak = lax.pmax(local_peak, "supp")
    factor = jnp.exp(local_peak - peak)
    partial_mix = both[:reps]
    drawn = counts > 0
    current = weights
    loglik = None
    for it in range(ITERS):
        if it > 0:
            hi, lo = split(current)
            pair = jnp.dot(jnp.concatenate([hi, lo], axis=0), tile, preferred_element_type=F32)
            partial_mix = pair[:reps] + pair[reps:]
        mixture = lax.psum(partial_mix * factor, "supp")
        if it == 0:
            loglik = (peak + jnp.log(mixture / total_supports) - log_scale[:1]) / samples
            loglik = loglik - 0.5 * math.log(2.0 * math.pi)
        resp = jnp.where(drawn, counts.astype(F32) / jnp.where(drawn, mixture, 1.0), 0.0) * factor
        hi, lo = split(resp)
        pair = lax.dot_general(jnp.concatenate([hi, lo], axis=0), tile, (((1,), (1,)), ((), ())),
                               preferred_element_type=F32)
        current = current * lax.psum(pair[:reps] + pair[reps:], "subj") / total_subjects
    return current, loglik


def body(observations, noise_scale, sample_times, counts, absorption, elimination, volume, weights):
    n_subj, n_supp = lax.axis_size("subj"), lax.axis_size("supp")
    subjects, samples = observations.shape
    sizes = (subjects * n_subj, weights.shape[1] * n_supp)
    inputs = (observations.T, noise_scale.T, sample_times.T,
              absorption[None, :], elimination[None, :], volume[None, :], weights)
    if (n_subj, n_supp) == (8, 4):
        new, loglik = run_em(*inputs, counts, 2, 4, sizes)
        return hand_over(pltpu.with_memory_space_constraint(new, pltpu.VMEM), pltpu.with_memory_space_constraint(loglik, pltpu.VMEM))
    return plain_em(*make_tile(*inputs), counts, weights, samples, *sizes)


def solution(mesh):
    return jax.shard_map(
        body,
        mesh=mesh,
        in_specs=(
            P("subj", None),
            P("subj", None),
            P("subj", None),
            P(None, "subj"),
            P("supp"),
            P("supp"),
            P("supp"),
            P(None, "supp"),
        ),
        out_specs=(P(None, "supp"), P(None, "subj")),
        check_vma=False,
    )
```
